32 devices in a mesh: dp: 8 (over z, y), seq: 4 (over x, core).
Axes of the slice: x: 2, y: 2, z: 4, core: 2. Of those that a mesh axis runs over, the one named last changes fastest.
Arguments:
- values: bfloat16 [8, 512, 8192], P('dp', 'seq'), may hold values from -6 to 6
- b_rows: bfloat16 [8, 512, 1024], P('dp', 'seq'), may hold values from -6 to 6
- c_rows: bfloat16 [8, 512, 1024], P('dp', 'seq'), may hold values from -0.03125 to 0.03125
- dt_rows: float32 [8, 512, 128], P('dp', 'seq'), may hold values from -2 to 2048
- a_log: float32 [128], P('seq'), as said below
- dt_bias: float32 [128], P('seq'), may hold values from -0.5 to 0.5
- d_skip: float32 [128], P('seq'), may hold values from 0.1 to 2.5
- cotangent: bfloat16 [8, 512, 8192], P('dp', 'seq'), may hold values from -6 to 6
Outputs:
- output: bfloat16 [8, 512, 8192], P('dp', 'seq')
- grad_x: bfloat16 [8, 512, 8192], P('dp', 'seq')
- grad_b: float32 [8, 512, 1024], P('dp', 'seq')
- grad_c: float32 [8, 512, 1024], P('dp', 'seq')
- grad_dt: float32 [8, 512, 128], P('dp', 'seq')
- grad_params: float32 [3, 128], P(None, 'seq')
The draws below stay inside these ranges and needn't reach their ends.
Inputs may be any that keep to these rules, and one draw needn't show every extreme that they name: The decay rates exp(a_log) lie between 1 / 2560 and 1 / 30.
All inputs are finite; a program needn't handle non-finite values.
Results may differ from the reference program's by a relative error of at most 0.011.
Values may be sent and summed in bfloat16 or wider, within the bound.
No kernel may reach another device: no remote copies, remote signals or barrier semaphores. Data moves between devices by JAX's collectives and lax.ppermute only.
A program may use at most 128 MiB of HBM per device.

```python
import math
import jax
import jax.numpy as jnp
from jax import lax

H = 128
G = 4
P_SIZE = 64
N = 256
SPAN = 128
LOCAL_TOKEN_SPAN = 128
SEQS = 8
SEQ_LEN = 512


def head_rates(key):
    leading_operand, trailing_operand, third = jax.random.split(jax.random.fold_in(key, 7), 3)
    share = 0.5
    slow_heads = jax.random.uniform(leading_operand, (H,), jnp.float32) < share
    slow_rate = jnp.exp(jax.random.uniform(trailing_operand, (H,), jnp.float32, math.log(0.2 / SEQ_LEN), math.log(0.8 / SEQ_LEN)))
    fast_rate = jnp.exp(jax.random.uniform(third, (H,), jnp.float32, math.log(1.0 / 50.0), math.log(1.0 / 30.0)))
    return jnp.where(slow_heads, slow_rate, fast_rate)


def transfer_arrangement(key):
    rates = head_rates(key)
    leading_operand, trailing_operand, third, fourth = jax.random.split(jax.random.fold_in(key, 11), 4)
    location_numbers = jax.random.randint(third, (SEQS, 2, 1), 0, SEQ_LEN)
    sequence_locations = jnp.arange(SEQ_LEN, dtype=jnp.int32)[None, None, :]
    head_group_lists = jnp.any(sequence_locations == location_numbers, axis=1)
    loss_values = jax.random.uniform(fourth, (SEQS, SEQ_LEN, H), jnp.float32, 0.25, 0.7)
    step_offsets = loss_values / rates
    return (head_group_lists, step_offsets, leading_operand, trailing_operand)


def draw_a_log(key, part):
    return jnp.log(head_rates(key)).astype(jnp.float32)


def draw_dt_rows(key, part):
    head_group_lists, step_offsets, leading_operand, trailing_operand = transfer_arrangement(key)
    random_perturbation = jnp.clip(0.5 * jax.random.normal(leading_operand, (SEQS, SEQ_LEN, H), jnp.float32), -1.5, 1.5)
    shifts = jax.random.uniform(trailing_operand, (SEQS, SEQ_LEN // LOCAL_TOKEN_SPAN, 1), jnp.float32, -0.7, 0.7)
    displacement_entries = jnp.repeat(shifts, LOCAL_TOKEN_SPAN, axis=1)
    return jnp.where(head_group_lists[:, :, None], step_offsets, 0.5 + displacement_entries + random_perturbation).astype(jnp.float32)


def draw_values(key, part):
    head_group_lists, step_offsets, leading_operand, trailing_operand = transfer_arrangement(key)
    sample_key = jax.random.fold_in(key, 23)
    sample_draw = jnp.clip(jax.random.normal(sample_key, (SEQS, SEQ_LEN, H, P_SIZE), jnp.float32), -6.0, 6.0)
    factor = jnp.where(head_group_lists[:, :, None], 1.0 / jnp.maximum(step_offsets, 1.0), 1.0)
    return (sample_draw * factor[:, :, :, None]).reshape(SEQS, SEQ_LEN, H * P_SIZE).astype(jnp.bfloat16)


def draw_b_rows(key, part):
    head_group_lists, step_offsets, leading_operand, trailing_operand = transfer_arrangement(key)
    sample_key = jax.random.fold_in(key, 29)
    sample_draw = jnp.clip(jax.random.normal(sample_key, (SEQS, SEQ_LEN, G * N), jnp.float32), -6.0, 6.0)
    factor = jnp.where(head_group_lists[:, :, None], 1.0 / SEQ_LEN, 1.0)
    return (sample_draw * factor).astype(jnp.bfloat16)


def levels(own_key, extent, cuts, low, largest):
    factor_of = 1.0
    for position, parts in cuts:
        draws = jax.random.uniform(jax.random.fold_in(jax.random.fold_in(own_key, 6), position), (parts,), jnp.float32, low / len(cuts), largest / len(cuts))
        factor_of = factor_of * jnp.repeat(jnp.exp(draws), extent[position] // parts).reshape((-1,) + (1,) * (len(extent) - 1 - position))
    return factor_of


def noise(rng, dims, deviation, limit, pieces=(), kind=jnp.bfloat16):
    entries = deviation * jax.random.normal(rng, dims, jnp.float32)
    if pieces:
        entries = entries * levels(rng, dims, pieces, -0.22, 0.18)
    return jnp.clip(entries, -limit, limit).astype(kind)


def setup_inputs(seed: int = 0) -> dict:
    arg_keys = jax.random.split(jax.random.key(seed), 9)
    return {
        "values": draw_values(jax.random.fold_in(arg_keys[8], 71), 0),
        "b_rows": draw_b_rows(jax.random.fold_in(arg_keys[8], 71), 0),
        "c_rows": noise(arg_keys[2], (SEQS, SEQ_LEN, G * N), (N * SPAN) ** -0.5, 0.03125, ((0, 8), (1, 4))),
        "dt_rows": draw_dt_rows(jax.random.fold_in(arg_keys[8], 71), 0),
        "a_log": draw_a_log(jax.random.fold_in(arg_keys[8], 71), 0),
        "dt_bias": jnp.clip(jax.random.uniform(arg_keys[5], (H,), jnp.float32, -0.5, 0.5) * levels(arg_keys[5], (H,), ((0, 4),), -0.4, 0.0), -0.5, 0.5),
        "d_skip": jnp.clip(0.1 + 2.4 * jax.random.uniform(arg_keys[6], (H,), jnp.float32) ** levels(arg_keys[6], (H,), ((0, 4),), -0.2, 0.2), 0.1, 2.5),
        "cotangent": noise(arg_keys[7], (SEQS, SEQ_LEN, H * P_SIZE), 1.0, 6.0, ((0, 8), (1, 4))),
    }


FULL_PRECISION = lax.Precision.HIGHEST

def mixer(values, b_rows, c_rows, dt_rows, a_log, dt_bias, d_skip):
    length, count_of_heads, head_size = values.shape
    blocks = length // SPAN
    step_rate = jax.nn.softplus(dt_rows + dt_bias)
    step_log = -step_rate * jnp.exp(a_log)
    cumul = jnp.cumsum(step_log.reshape(blocks, SPAN, count_of_heads).transpose(2, 0, 1), axis=2)
    rows_at = lax.broadcasted_iota(jnp.int32, (SPAN, SPAN), 0)
    cols_at = lax.broadcasted_iota(jnp.int32, (SPAN, SPAN), 1)
    causal = rows_at >= cols_at
    gap_log = cumul[:, :, :, None] - cumul[:, :, None, :]
    decays = jnp.where(causal, jnp.exp(jnp.where(causal, gap_log, 0.0)), 0.0)
    blocked = values.reshape(blocks, SPAN, count_of_heads, head_size)
    scaled_full = blocked * step_rate.reshape(blocks, SPAN, count_of_heads)[:, :, :, None]
    scaled = scaled_full.astype(jnp.bfloat16)
    b_block = b_rows.reshape(blocks, SPAN, -1).astype(jnp.bfloat16)
    c_block = c_rows.reshape(blocks, SPAN, -1).astype(jnp.bfloat16)
    scores = jnp.einsum('cin,cjn->cij', c_block, b_block, preferred_element_type=jnp.float32)
    mixing = (scores[None] * decays).astype(jnp.bfloat16)
    intra_out = jnp.einsum('hcij,cjhp->cihp', mixing, scaled, preferred_element_type=jnp.float32)
    tail_log = cumul[:, :, -1]
    weights = jnp.exp(tail_log[:, :, None] - cumul)
    weighted = (scaled_full * weights.transpose(1, 2, 0)[:, :, :, None]).astype(jnp.bfloat16)
    block_state = jnp.einsum('cjhp,cjn->chpn', weighted, b_block, preferred_element_type=jnp.float32)
    end_logs = jnp.cumsum(tail_log, axis=1)
    before = end_logs - tail_log
    after_block = lax.broadcasted_iota(jnp.int32, (blocks, blocks), 0) > lax.broadcasted_iota(jnp.int32, (blocks, blocks), 1)
    carry_gap = before[:, :, None] - end_logs[:, None, :]
    carry_decay = jnp.where(after_block, jnp.exp(jnp.where(after_block, carry_gap, 0.0)), 0.0)
    entering = jnp.einsum('hkc,chpn->khpn', carry_decay, block_state, precision=FULL_PRECISION).astype(jnp.bfloat16)
    reached = jnp.einsum('kin,khpn->kihp', c_block, entering, preferred_element_type=jnp.float32)
    inter_out = reached * jnp.exp(cumul).transpose(1, 2, 0)[:, :, :, None]
    final_output = intra_out + inter_out + d_skip[:, None] * blocked
    return final_output.reshape(length, count_of_heads, head_size)

def group_pass(operands):
    values, b_rows, c_rows, dt_rows, a_log, dt_bias, d_skip, cotangent = operands
    final_output, pullback = jax.vjp(mixer, values.astype(jnp.float32), b_rows.astype(jnp.float32), c_rows.astype(jnp.float32), dt_rows, a_log, dt_bias, d_skip)
    gradients = pullback(cotangent.astype(jnp.float32))
    return (final_output.astype(jnp.bfloat16), gradients[0].astype(jnp.bfloat16), gradients[1], gradients[2], gradients[3], gradients[4], gradients[5], gradients[6])

def reference(values, b_rows, c_rows, dt_rows, a_log, dt_bias, d_skip, cotangent):
    per_group = H // G

    def by_group(source, column_entries):
        return source.reshape(SEQS, SEQ_LEN, G, column_entries).transpose(0, 2, 1, 3).reshape(SEQS * G, SEQ_LEN, column_entries)

    def tiled(parameter):
        return jnp.tile(parameter.reshape(G, per_group), (SEQS, 1))

    def back(source, column_entries):
        return source.reshape(SEQS, G, SEQ_LEN, column_entries).transpose(0, 2, 1, 3).reshape(SEQS, SEQ_LEN, G * column_entries)
    head_vals = by_group(values, per_group * P_SIZE).reshape(SEQS * G, SEQ_LEN, per_group, P_SIZE)
    head_cot = by_group(cotangent, per_group * P_SIZE).reshape(SEQS * G, SEQ_LEN, per_group, P_SIZE)
    head_b = by_group(b_rows, N)
    head_c = by_group(c_rows, N)
    head_dt = by_group(dt_rows, per_group)
    results = lax.map(group_pass, (head_vals, head_b, head_c, head_dt, tiled(a_log), tiled(dt_bias), tiled(d_skip), head_cot))
    output = back(results[0].reshape(SEQS * G, SEQ_LEN, per_group * P_SIZE), per_group * P_SIZE)
    grad_x = back(results[1].reshape(SEQS * G, SEQ_LEN, per_group * P_SIZE), per_group * P_SIZE)
    grad_b = back(results[2], N)
    grad_c = back(results[3], N)
    grad_dt = back(results[4], per_group)
    grad_params = jnp.stack([results[5].reshape(SEQS, H).sum(axis=0), results[6].reshape(SEQS, H).sum(axis=0), results[7].reshape(SEQS, H).sum(axis=0)])
    return (output, grad_x, grad_b, grad_c, grad_dt, grad_params)
```

```python
import functools

import jax
import jax.numpy as jnp
from jax import lax
from jax.experimental import pallas as pl
from jax.experimental.pallas import tpu as pltpu
from jax.sharding import PartitionSpec as P

H = 128
G = 4
P_SIZE = 64
N = 256
SPAN = 128
PER_GROUP = H // G
WIDTH = PER_GROUP * P_SIZE
PAIR = 2 * P_SIZE
PAIRS = PER_GROUP // 2
TILE = 512
VMEM_LIMIT = 24 * 1024 * 1024

F32 = jnp.float32
BF16 = jnp.bfloat16
NN = (((1,), (0,)), ((), ()))
NT = (((1,), (1,)), ((), ()))
TN = (((0,), (0,)), ((), ()))


def dot(left, right, dims=NN, precision=None):
    return lax.dot_general(left, right, dims, precision=precision, preferred_element_type=F32)


def split(a):
    high = a.astype(BF16)
    low = (a - high.astype(F32)).astype(BF16)
    return jnp.concatenate([high, low], axis=1)


def spread(rows, width):
    head = lax.broadcasted_iota(jnp.int32, (rows, width), 0) & (PER_GROUP - 1)
    lane = lax.broadcasted_iota(jnp.int32, (rows, width), 1) >> 6
    return jnp.where(head == lane, 1.0, 0.0).astype(BF16)


def over_lanes(a, spreader):
    return dot(split(a), spreader)


def per_head(a, spreader):
    high = a.astype(BF16)
    low = (a - high.astype(F32)).astype(BF16)
    return dot(high, spreader, NT) + dot(low, spreader, NT)


def decays(raw, decay_rate):
    rate = jnp.maximum(raw, 0.0) + jnp.log1p(jnp.exp(-jnp.abs(raw)))
    at_row = lax.broadcasted_iota(jnp.int32, (SPAN, SPAN), 0)
    at_col = lax.broadcasted_iota(jnp.int32, (SPAN, SPAN), 1)
    lower = jnp.where(at_row >= at_col, 1.0, 0.0)
    cum = dot(lower, -rate * decay_rate, precision=lax.Precision.HIGHEST)
    tail = cum[SPAN - 1 : SPAN, :]
    wide = jnp.exp(jnp.minimum(tail - cum, 0.0)) * rate
    return rate, cum, tail, wide, jnp.exp(cum)


def prepare(flag_ref, dt_ref, near_ref, param_ref, *refs):
    rate_ref, wide_ref, grow_ref, cum_ref, cumt_ref, slope_ref, other_ref, rows_ref, spread_ref = refs[-9:]
    spread_ref[...] = spread(2 * PER_GROUP, WIDTH)
    params = param_ref[...]
    decay_rate = jnp.exp(params[0:1, :])
    raw = dt_ref[...] + params[1:2, :]
    rate, cum, tail, wide, grow = decays(raw, decay_rate)
    rate_ref[...] = rate
    wide_ref[...] = wide
    grow_ref[...] = grow
    cum_ref[...] = cum
    cumt_ref[...] = cum.T
    small = jnp.exp(-jnp.abs(raw))
    slope_ref[...] = jnp.where(raw >= 0.0, 1.0, small) / (1.0 + small)
    _, _, near_tail, near_wide, near_grow = decays(near_ref[:SPAN, :] + params[1:2, :], decay_rate)
    other_ref[...] = jnp.where(flag_ref[2] == 1, near_wide, near_grow)
    rows_ref[...] = jnp.concatenate(
        [jnp.exp(tail), decay_rate, params[2:3, :], jnp.exp(near_tail), jnp.zeros((4, H), F32)], axis=0
    )


def carry_state(
    g, carried, flag_ref, x_ref, dy_ref, b_ref, c_ref, wide_ref, grow_ref, rows_ref, spread_ref, *refs
):
    sent_ref = refs[-1]

    @pl.when(flag_ref[1] == 1)
    def _():
        forward = flag_ref[0] == 1
        heads = slice(g * PER_GROUP, (g + 1) * PER_GROUP)
        factor = jnp.where(forward, wide_ref[:, heads], grow_ref[:, heads])
        own_rows = jnp.where(
            forward, b_ref[:, g * N : (g + 1) * N], c_ref[:, g * N : (g + 1) * N]
        )
        spreader = spread_ref
        factor_hl = split(factor)
        decay_hl = split(jnp.broadcast_to(rows_ref[0:1, heads], (8, PER_GROUP)))
        for lo in range(0, WIDTH, TILE):
            lanes = slice(lo, lo + TILE)
            wide = slice(g * WIDTH + lo, g * WIDTH + lo + TILE)
            inputs = jnp.where(forward, x_ref[:, wide], dy_ref[:, wide]).astype(F32)
            weighted = (inputs * dot(factor_hl, spreader[:, lanes])).astype(BF16)
            state = dot(own_rows, weighted, TN)
            if carried:
                arrived = refs[0][:, lanes].astype(F32)
                for more in refs[1:-1]:
                    arrived = arrived + more[:, lanes].astype(F32)
                decay = dot(decay_hl, spreader[:, lanes])[0:1, :]
                state = state + arrived * decay
            sent_ref[:, lanes] = state.astype(BF16)


def pair_state(
    g, flag_ref, x_ref, dy_ref, b_ref, c_ref, near_in_ref, near_rows_ref, wide_ref, grow_ref,
    other_ref, rows_ref, spread_ref, near_ref, sent_ref,
):
    onward = flag_ref[2] == 1
    heads = slice(g * PER_GROUP, (g + 1) * PER_GROUP)
    rows = slice(g * N, (g + 1) * N)
    wide = slice(g * WIDTH, (g + 1) * WIDTH)
    near_in = near_in_ref[:, wide].astype(F32) * over_lanes(other_ref[:, heads], spread_ref[...])
    near_term = dot(near_rows_ref[:, rows], near_in.astype(BF16), TN)
    near_ref[...] = near_term.astype(BF16)

    @pl.when(flag_ref[1] == 1)
    def _():
        own_rows = jnp.where(onward, b_ref[:, rows], c_ref[:, rows])
        own_in = jnp.where(onward, x_ref[:, wide], dy_ref[:, wide]).astype(F32)
        factor = jnp.where(onward, wide_ref[:, heads], grow_ref[:, heads])
        own_in = (own_in * over_lanes(factor, spread_ref[...])).astype(BF16)
        decay = over_lanes(jnp.broadcast_to(rows_ref[0:1, heads], (8, PER_GROUP)), spread_ref[...])
        sent_ref[...] = (dot(own_rows, own_in, TN) + near_term * decay[0:1, :]).astype(BF16)


def within_block(
    g, x_ref, dy_ref, b_ref, c_ref, rate_ref, cum_ref, cumt_ref, rows_ref, spread_ref,
    outp_ref, dxp_ref, db_ref, dc_ref, gap_ref, direct_ref, skip_ref, gap_s, direct_s, skip_s,
):
    heads = slice(g * PER_GROUP, (g + 1) * PER_GROUP)
    spreader = spread_ref
    rate_hl = split(rate_ref[:, heads])
    skip_hl = split(jnp.broadcast_to(rows_ref[2:3, heads], (8, PER_GROUP)))
    at_row = lax.broadcasted_iota(jnp.int32, (SPAN, SPAN), 0)
    at_col = lax.broadcasted_iota(jnp.int32, (SPAN, SPAN), 1)
    causal = at_row >= at_col
    first = lax.broadcasted_iota(jnp.int32, (SPAN, PAIR), 1) < P_SIZE
    b_rows, c_rows = b_ref[:, g * N : (g + 1) * N], c_ref[:, g * N : (g + 1) * N]
    scores = jnp.where(causal, dot(c_rows, b_rows, NT), 0.0)
    dscores = jnp.zeros((SPAN, SPAN), F32)
    for j in range(PAIRS):
        lanes = slice(j * PAIR, (j + 1) * PAIR)
        head = g * PER_GROUP + 2 * j
        wide = slice(g * WIDTH + j * PAIR, g * WIDTH + (j + 1) * PAIR)
        x = x_ref[:, wide].astype(F32)
        dy = dy_ref[:, wide]
        rate = dot(rate_hl, spreader[:, lanes])
        skip = dot(skip_hl, spreader[:, lanes])[0:1, :]
        scaled = x * rate
        both = jnp.concatenate(
            [jnp.where(first, scaled, 0.0), jnp.where(first, 0.0, scaled)], axis=0
        ).astype(BF16)
        scaled = scaled.astype(BF16).astype(F32)
        decays = [
            jnp.exp(jnp.minimum(cum_ref[:, h : h + 1] - cumt_ref[h : h + 1, :], 0.0))
            for h in (head, head + 1)
        ]
        mixing = jnp.concatenate([(scores * d).astype(BF16) for d in decays], axis=1)
        intra = dot(mixing, both)
        dmixing = dot(dy, both, NT)
        dscores = dscores + (dmixing[:, :SPAN] * decays[0] + dmixing[:, SPAN:] * decays[1])
        crossed = dot(mixing, dy, TN)
        dscaled = jnp.where(first, crossed[:SPAN], crossed[SPAN:])
        dy = dy.astype(F32)
        direct = scaled * dscaled
        outp_ref[:, lanes] = intra + skip * x
        dxp_ref[:, lanes] = dscaled * rate + skip * dy
        gap_s[:, lanes] = dy * intra - direct
        direct_s[:, lanes] = direct
        skip_s[:, lanes] = jnp.sum((dy * x).reshape(SPAN // 8, 8, PAIR), axis=0)
    dscores = jnp.where(causal, dscores, 0.0).astype(BF16)
    dc_ref[...] = dot(dscores, b_rows)
    db_ref[...] = dot(dscores, c_rows, TN)
    one = spreader[:PER_GROUP, :]
    gap_ref[...] = per_head(gap_s[...], one)
    direct_ref[...] = per_head(direct_s[...], one)
    skip_ref[...] = per_head(skip_s[...], one)


def across_blocks(
    g, flag_ref, x_ref, dy_ref, b_ref, c_ref, rate_ref, wide_ref, grow_ref, slope_ref, rows_ref, spread_ref,
    dbp_ref, dcp_ref, gap_ref, direct_ref, skip_ref, outp_ref, dxp_ref, near_ref, crossed_ref, passed_ref, *refs,
):
    earlier = refs[:6] if g else ()
    out_ref, dx_ref, db_ref, dc_ref, ddt_ref, par_ref = refs[len(earlier) : len(earlier) + 6]
    out_s, dx_s, rows_s, out_sems, rows_sems = refs[len(earlier) + 6 :]
    forward = flag_ref[0] == 1
    inner = flag_ref[1] == 1

    def moves(k):
        lanes = pl.ds(k * TILE, TILE)
        wide = pl.ds(g * WIDTH + k * TILE, TILE)
        pairs = [(out_s.at[:, lanes], out_ref.at[:, wide]), (dx_s.at[:, lanes], dx_ref.at[:, wide])]
        return [pltpu.make_async_copy(a, b, out_sems.at[i, k]) for i, (a, b) in enumerate(pairs)]

    def rows_moves():
        lanes = pl.ds(g * N, N)
        pairs = [(rows_s.at[0], db_ref.at[:, lanes]), (rows_s.at[1], dc_ref.at[:, lanes])]
        return [pltpu.make_async_copy(a, b, rows_sems.at[i]) for i, (a, b) in enumerate(pairs)]

    heads = slice(g * PER_GROUP, (g + 1) * PER_GROUP)
    spreader = spread_ref
    one = spreader[:PER_GROUP, :]
    wide_hl = split(wide_ref[:, heads])
    grow_hl = split(grow_ref[:, heads])
    decay_hl = split(jnp.broadcast_to(rows_ref[3:4, heads], (8, PER_GROUP)))
    b_rows, c_rows = b_ref[:, g * N : (g + 1) * N], c_ref[:, g * N : (g + 1) * N]
    dc = dcp_ref[...]
    db = dbp_ref[...]
    gap = gap_ref[...]
    tail_in = jnp.zeros((SPAN, PER_GROUP), F32)
    product = jnp.zeros((8, PER_GROUP), F32)
    for k in range(WIDTH // TILE):
        lanes = slice(k * TILE, (k + 1) * TILE)
        wide_lanes = slice(g * WIDTH + k * TILE, g * WIDTH + (k + 1) * TILE)
        near_term = near_ref[:, lanes]
        far_term = jnp.where(inner, crossed_ref[:, lanes], passed_ref[:, lanes])
        decay = dot(decay_hl, spreader[:, lanes])[0:1, :]
        joined = (far_term.astype(F32) * decay + near_term.astype(F32)).astype(BF16)
        first = jnp.where(inner, near_term, jnp.zeros_like(near_term))
        second = jnp.where(inner, far_term, joined)
        enter = jnp.where(forward, first, second)
        leave = jnp.where(forward, second, first)
        x = x_ref[:, wide_lanes].astype(F32)
        dy = dy_ref[:, wide_lanes].astype(F32)
        grow = dot(grow_hl, spreader[:, lanes])
        wide = dot(wide_hl, spreader[:, lanes])
        inter = dot(c_rows, enter) * grow
        out_s[:, lanes] = (outp_ref[:, lanes] + inter).astype(BF16)
        dc = dc + dot((dy * grow).astype(BF16), enter, NT)
        dweighted = dot(b_rows, leave)
        weighted = (x * wide).astype(BF16)
        db = db + dot(weighted, leave, NT)
        dx_s[:, lanes] = (dxp_ref[:, lanes] + wide * dweighted).astype(BF16)
        for move in moves(k):
            move.start()
        tail_term = weighted.astype(F32) * dweighted
        gap = gap + per_head(dy * inter - tail_term, one[:, lanes])
        tail_in = tail_in + per_head(tail_term, one[:, lanes])
        both = enter.astype(F32) * leave.astype(F32)
        product = product + per_head(jnp.sum(both.reshape(N // 8, 8, TILE), axis=0), one[:, lanes])
    rows_s[0] = db
    rows_s[1] = dc
    for move in rows_moves():
        move.start()
    rate = rate_ref[:, heads]
    decay_rate = rows_ref[1:2, heads]
    dtail = jnp.sum(tail_in, axis=0, keepdims=True) + rows_ref[0:1, heads] * jnp.sum(
        product, axis=0, keepdims=True
    )
    at_row = lax.broadcasted_iota(jnp.int32, (SPAN, SPAN), 0)
    at_col = lax.broadcasted_iota(jnp.int32, (SPAN, SPAN), 1)
    upper = jnp.where(at_row <= at_col, 1.0, 0.0)
    dlog = dot(upper, gap, precision=lax.Precision.HIGHEST) + dtail
    drate = (direct_ref[...] + tail_in) / rate - decay_rate * dlog
    ddt = drate * slope_ref[:, heads]
    da = -decay_rate * jnp.sum(rate * dlog, axis=0, keepdims=True)
    dbias = jnp.sum(ddt, axis=0, keepdims=True)
    dskip = jnp.sum(skip_ref[...], axis=0, keepdims=True)
    pad = jnp.zeros((5, PER_GROUP), F32)
    par = jnp.concatenate([da, dbias, dskip, pad], axis=0)
    if g == 0:
        ddt_ref[...] = jnp.zeros((SPAN, H), F32)
        par_ref[...] = jnp.zeros((8, H), F32)
    else:
        ddt_ref[...] = earlier[2][...]
        par_ref[...] = earlier[3][...]
    ddt_ref[:, heads] = ddt
    par_ref[:, heads] = par
    for k in range(WIDTH // TILE):
        for move in moves(k):
            move.wait()
    for move in rows_moves():
        move.wait()


SCALARS = pl.BlockSpec(memory_space=pltpu.SMEM)
ANYWHERE = pl.BlockSpec(memory_space=pl.ANY)
PARAMS = pltpu.CompilerParams(vmem_limit_bytes=VMEM_LIMIT)
ON_CHIP = pl.BlockSpec(memory_space=pltpu.VMEM)


def cost(flops, moved):
    return pl.CostEstimate(flops=int(flops), bytes_accessed=int(moved), transcendentals=0)


def call_prepare(flags, dt_rows, near_dt, params, data):
    square = jax.ShapeDtypeStruct((SPAN, H), F32)
    return pl.pallas_call(
        prepare,
        in_specs=[SCALARS] + [ON_CHIP] * 7,
        out_specs=[ON_CHIP] * 9,
        out_shape=[square] * 7
        + [jax.ShapeDtypeStruct((8, H), F32), jax.ShapeDtypeStruct((2 * PER_GROUP, WIDTH), BF16)],
        compiler_params=PARAMS,
        cost_estimate=cost(3e7, 6e5),
        name="prepare",
    )(flags, dt_rows, near_dt, params, *data)


def call_pair(g, flags, data, near, prep):
    _, wide, grow, _, _, _, other, rows, spreader = prep
    state = jax.ShapeDtypeStruct((N, WIDTH), BF16)
    return pl.pallas_call(
        functools.partial(pair_state, g),
        in_specs=[SCALARS] + [ON_CHIP] * 11,
        out_specs=[ON_CHIP] * 2,
        out_shape=[state] * 2,
        compiler_params=PARAMS,
        cost_estimate=cost(3e8, 4e6),
        name=f"pair{g}",
    )(flags, *data, *near, wide, grow, other, rows, spreader)


def call_carry(g, flags, data, prep, arrived):
    values, cot, b_rows, c_rows = data
    _, wide, grow, _, _, _, _, rows, spreader = prep
    return pl.pallas_call(
        functools.partial(carry_state, g, bool(arrived)),
        in_specs=[SCALARS] + [ON_CHIP] * (8 + len(arrived)),
        out_specs=ON_CHIP,
        out_shape=jax.ShapeDtypeStruct((N, WIDTH), BF16),
        compiler_params=PARAMS,
        cost_estimate=cost(1.6e8, 3e6),
        name=f"carry{g}",
    )(flags, values, cot, b_rows, c_rows, wide, grow, rows, spreader, *arrived)


def call_within(g, data, prep):
    values, cot, b_rows, c_rows = data
    rate, _, _, cum, cumt, _, _, rows, spreader = prep
    wide_shape = jax.ShapeDtypeStruct((SPAN, WIDTH), F32)
    rows_shape = jax.ShapeDtypeStruct((SPAN, N), F32)
    head_shape = jax.ShapeDtypeStruct((SPAN, PER_GROUP), F32)
    return pl.pallas_call(
        functools.partial(within_block, g),
        in_specs=[ON_CHIP] * 9,
        out_specs=[ON_CHIP] * 7,
        out_shape=[wide_shape] * 2
        + [rows_shape] * 2
        + [head_shape] * 2
        + [jax.ShapeDtypeStruct((8, PER_GROUP), F32)],
        scratch_shapes=[pltpu.VMEM((SPAN, WIDTH), F32)] * 2 + [pltpu.VMEM((8, WIDTH), F32)],
        compiler_params=PARAMS,
        cost_estimate=cost(1.5e9, 4e6),
        name=f"within{g}",
    )(values, cot, b_rows, c_rows, rate, cum, cumt, rows, spreader)


def call_across(g, flags, data, prep, local, states, so_far):
    values, cot, b_rows, c_rows = data
    rate, wide, grow, _, _, slope, _, rows, spreader = prep
    outp, dxp, dbp, dcp, gap, direct, skip = local
    tokens, features = values.shape
    n_in = 21
    if so_far is None:
        earlier, specs, aliases = (), [], {}
    else:
        out, dx, db, dc, ddt, par = so_far
        earlier = (out, dx, ddt, par, db, dc)
        specs = [ANYWHERE, ANYWHERE, ON_CHIP, ON_CHIP, ANYWHERE, ANYWHERE]
        aliases = {n_in: 0, n_in + 1: 1, n_in + 2: 4, n_in + 3: 5, n_in + 4: 2, n_in + 5: 3}
    tiles = WIDTH // TILE
    return pl.pallas_call(
        functools.partial(across_blocks, g),
        in_specs=[SCALARS] + [ON_CHIP] * 20 + specs,
        out_specs=[ANYWHERE] * 4 + [ON_CHIP] * 2,
        out_shape=[jax.ShapeDtypeStruct((tokens, features), BF16)] * 2
        + [jax.ShapeDtypeStruct((tokens, G * N), F32)] * 2
        + [jax.ShapeDtypeStruct((tokens, H), F32), jax.ShapeDtypeStruct((8, H), F32)],
        scratch_shapes=[pltpu.VMEM((SPAN, WIDTH), BF16)] * 2
        + [pltpu.VMEM((2, SPAN, N), F32)]
        + [pltpu.SemaphoreType.DMA((2, tiles)), pltpu.SemaphoreType.DMA((2,))],
        input_output_aliases=aliases,
        compiler_params=PARAMS,
        cost_estimate=cost(6e8, 6e6),
        name=f"across{g}",
    )(flags, values, cot, b_rows, c_rows, rate, wide, grow, slope, rows, spreader,
      dbp, dcp, gap, direct, skip, outp, dxp, *states, *earlier)


def per_device(values, b_rows, c_rows, dt_rows, a_log, dt_bias, d_skip, cotangent):
    ranks = lax.axis_size("seq")
    copies = lax.axis_size("dp")
    rank = lax.axis_index("seq")
    tokens = values.shape[1]
    mine = a_log.shape[0]
    data = (
        values.reshape(tokens, H * P_SIZE),
        cotangent.reshape(tokens, H * P_SIZE),
        b_rows.reshape(tokens, G * N),
        c_rows.reshape(tokens, G * N),
    )
    own = jnp.concatenate([jnp.stack([a_log, dt_bias, d_skip]), jnp.zeros((5, mine), F32)], axis=0)
    at_lane = lax.broadcasted_iota(jnp.int32, (8, H), 1) // mine
    own = jnp.where(at_lane == rank, jnp.tile(own, (1, ranks)), 0.0)
    own_dt = dt_rows.reshape(tokens, H)
    half = ranks // 2
    forward = rank < half
    depth = jnp.where(forward, rank, ranks - 1 - rank)

    def flags(*bits):
        return jnp.stack([jnp.asarray(bit) for bit in bits]).astype(jnp.int32)

    def both_ways(step):
        return [(step, step + 1), (ranks - 1 - step, ranks - 2 - step)]

    if ranks == 4:
        marks = flags(forward, depth == 1, rank % 2 == 1)
        swap = [(i, i ^ 1) for i in range(ranks)]
        even = rank % 2 == 0
        near_dt = lax.ppermute(jnp.concatenate([own_dt, own], axis=0), "seq", swap)
        near = (
            lax.ppermute(jnp.where(even, data[0], data[1]), "seq", swap),
            lax.ppermute(jnp.where(even, data[2], data[3]), "seq", swap),
        )
        params = own + near_dt[SPAN:]
        params = params + lax.ppermute(params, "seq", [(i, i ^ 2) for i in range(ranks)])
        prep = call_prepare(marks, own_dt, near_dt, params, data)
        pairs = [call_pair(g, marks, data, near, prep) for g in range(G)]
        crossed = [lax.ppermute(sent, "seq", both_ways(1)) for _, sent in pairs]
        local, token, result = [], pairs[G - 1][0], None
        for g in range(G):
            rows, _ = lax.optimization_barrier((prep[7], token))
            local.append(call_within(g, data, (*prep[:7], rows, prep[8])))
            token = local[g][-1]

        def pass_on(g, token):
            arrived, _ = lax.optimization_barrier((crossed[g], token))
            return pairs[g][0], arrived, lax.ppermute(arrived, "seq", both_ways(2))

        states = [pass_on(0, prep[7]), pass_on(1, local[0][-1]), pass_on(2, local[3][-1])]
        result = call_across(0, marks, data, prep, local[0], states[0], None)
        result = call_across(1, marks, data, prep, local[1], states[1], result)
        states.append(pass_on(3, result[-1]))
        for g in (2, 3):
            result = call_across(g, marks, data, prep, local[g], states[g], result)
    else:
        marks = flags(forward, True, True)
        params = lax.psum(own, "seq")
        prep = call_prepare(marks, own_dt, own_dt, params, data)
        states = []
        for g in range(G):
            first = None
            for step in range(half):
                arrived = () if first is None else (first,)
                sent = call_carry(g, flags(forward, depth == step), data, prep, arrived)
                got = lax.ppermute(sent, "seq", both_ways(step))
                if step < half - 1:
                    first = got if first is None else first + got
            for step in range(half, ranks - 1):
                role = flags(jnp.logical_not(forward), depth == ranks - 1 - step)
                sent = call_carry(g, role, data, prep, (got,))
                got = got + lax.ppermute(sent, "seq", both_ways(step))
            states.append((jnp.zeros_like(got) if first is None else first, got, got))
        result = None
        for g in range(G):
            local = call_within(g, data, prep)
            result = call_across(g, marks, data, prep, local, states[g], result)
    out, dx, db, dc, ddt, par = result
    for axis, size in (("seq", ranks), ("dp", copies)):
        hop = 1
        while hop < size:
            par = par + lax.ppermute(par, axis, [(i, i ^ hop) for i in range(size)])
            hop *= 2
    grad_params = lax.dynamic_slice_in_dim(par, rank * mine, mine, 1)[:3]
    return (
        out.reshape(1, tokens, H * P_SIZE),
        dx.reshape(1, tokens, H * P_SIZE),
        db.reshape(1, tokens, G * N),
        dc.reshape(1, tokens, G * N),
        ddt.reshape(1, tokens, H),
        grad_params,
    )


def solution(mesh):
    rows = P("dp", "seq", None)
    heads = P("seq")
    return jax.shard_map(
        per_device,
        mesh=mesh,
        in_specs=(rows, rows, rows, rows, heads, heads, heads, rows),
        out_specs=(rows, rows, rows, rows, rows, P(None, "seq")),
        check_vma=False,
    )
```

```python
import functools

import jax
import jax.numpy as jnp
from jax import lax
from jax.experimental import pallas as pl
from jax.experimental.pallas import tpu as pltpu
from jax.sharding import PartitionSpec as P

H = 128
G = 4
P_SIZE = 64
N = 256
SPAN = 128
PER_GROUP = H // G
WIDTH = PER_GROUP * P_SIZE
PAIR = 2 * P_SIZE
PAIRS = PER_GROUP // 2
TILE = 512
VMEM_LIMIT = 24 * 1024 * 1024

F32 = jnp.float32
BF16 = jnp.bfloat16
NN = (((1,), (0,)), ((), ()))
NT = (((1,), (1,)), ((), ()))
TN = (((0,), (0,)), ((), ()))


def dot(left, right, dims=NN, precision=None):
    return lax.dot_general(left, right, dims, precision=precision, preferred_element_type=F32)


def split(a):
    high = a.astype(BF16)
    low = (a - high.astype(F32)).astype(BF16)
    return jnp.concatenate([high, low], axis=1)


def spread(rows, width):
    head = lax.broadcasted_iota(jnp.int32, (rows, width), 0) & (PER_GROUP - 1)
    lane = lax.broadcasted_iota(jnp.int32, (rows, width), 1) >> 6
    return jnp.where(head == lane, 1.0, 0.0).astype(BF16)


def over_lanes(a, spreader):
    return dot(split(a), spreader)


def per_head(a, spreader):
    high = a.astype(BF16)
    low = (a - high.astype(F32)).astype(BF16)
    return dot(high, spreader, NT) + dot(low, spreader, NT)


def decays(raw, decay_rate):
    rate = jnp.maximum(raw, 0.0) + jnp.log1p(jnp.exp(-jnp.abs(raw)))
    at_row = lax.broadcasted_iota(jnp.int32, (SPAN, SPAN), 0)
    at_col = lax.broadcasted_iota(jnp.int32, (SPAN, SPAN), 1)
    lower = jnp.where(at_row >= at_col, 1.0, 0.0)
    cum = dot(lower, -rate * decay_rate, precision=lax.Precision.HIGHEST)
    tail = cum[SPAN - 1 : SPAN, :]
    wide = jnp.exp(jnp.minimum(tail - cum, 0.0)) * rate
    return rate, cum, tail, wide, jnp.exp(cum)


def lay_out(spread_ref):
    spread_ref[...] = spread(2 * PER_GROUP, WIDTH)


def prepare(flag_ref, dt_ref, near_ref, param_ref, *refs):
    rate_ref, wide_ref, grow_ref, cum_ref, cumt_ref, slope_ref, other_ref, rows_ref = refs[-8:]
    params = param_ref[...]
    decay_rate = jnp.exp(params[0:1, :])
    raw = dt_ref[...] + params[1:2, :]
    rate, cum, tail, wide, grow = decays(raw, decay_rate)
    rate_ref[...] = rate
    wide_ref[...] = wide
    grow_ref[...] = grow
    cum_ref[...] = cum
    cumt_ref[...] = cum.T
    small = jnp.exp(-jnp.abs(raw))
    slope_ref[...] = jnp.where(raw >= 0.0, 1.0, small) / (1.0 + small)
    _, _, near_tail, near_wide, near_grow = decays(near_ref[:SPAN, :] + params[1:2, :], decay_rate)
    other_ref[...] = jnp.where(flag_ref[2] == 1, near_wide, near_grow)
    rows_ref[...] = jnp.concatenate(
        [jnp.exp(tail), decay_rate, params[2:3, :], jnp.exp(near_tail), jnp.zeros((4, H), F32)], axis=0
    )


def carry_state(
    g, carried, flag_ref, x_ref, dy_ref, b_ref, c_ref, wide_ref, grow_ref, rows_ref, spread_ref, *refs
):
    sent_ref = refs[-1]

    @pl.when(flag_ref[1] == 1)
    def _():
        forward = flag_ref[0] == 1
        heads = slice(g * PER_GROUP, (g + 1) * PER_GROUP)
        factor = jnp.where(forward, wide_ref[:, heads], grow_ref[:, heads])
        own_rows = jnp.where(
            forward, b_ref[:, g * N : (g + 1) * N], c_ref[:, g * N : (g + 1) * N]
        )
        spreader = spread_ref
        factor_hl = split(factor)
        decay_hl = split(jnp.broadcast_to(rows_ref[0:1, heads], (8, PER_GROUP)))
        for lo in range(0, WIDTH, TILE):
            lanes = slice(lo, lo + TILE)
            wide = slice(g * WIDTH + lo, g * WIDTH + lo + TILE)
            inputs = jnp.where(forward, x_ref[:, wide], dy_ref[:, wide]).astype(F32)
            weighted = (inputs * dot(factor_hl, spreader[:, lanes])).astype(BF16)
            state = dot(own_rows, weighted, TN)
            if carried:
                arrived = refs[0][:, lanes].astype(F32)
                for more in refs[1:-1]:
                    arrived = arrived + more[:, lanes].astype(F32)
                decay = dot(decay_hl, spreader[:, lanes])[0:1, :]
                state = state + arrived * decay
            sent_ref[:, lanes] = state.astype(BF16)


def pair_state(
    groups, start, flag_ref, x_ref, dy_ref, b_ref, c_ref, near_in_ref, near_rows_ref, wide_ref, grow_ref,
    other_ref, rows_ref, spread_ref, near_ref, sent_ref,
):
    onward = flag_ref[2] == 1
    for k, g in enumerate(groups):
        heads = slice(g * PER_GROUP, (g + 1) * PER_GROUP)
        rows = slice(g * N, (g + 1) * N)
        wide = slice(g * WIDTH, (g + 1) * WIDTH)
        to = slice(k * WIDTH, (k + 1) * WIDTH)
        near_in = near_in_ref[:, (g - start) * WIDTH : (g - start + 1) * WIDTH].astype(F32) * over_lanes(other_ref[:, heads], spread_ref[...])
        near_term = dot(near_rows_ref[:, rows], near_in.astype(BF16), TN)
        near_ref[:, to] = near_term.astype(BF16)

        @pl.when(flag_ref[1] == 1)
        def _(near_term=near_term, heads=heads, rows=rows, wide=wide, to=to):
            own_rows = jnp.where(onward, b_ref[:, rows], c_ref[:, rows])
            own_in = jnp.where(onward, x_ref[:, wide], dy_ref[:, wide]).astype(F32)
            factor = jnp.where(onward, wide_ref[:, heads], grow_ref[:, heads])
            own_in = (own_in * over_lanes(factor, spread_ref[...])).astype(BF16)
            decay = over_lanes(jnp.broadcast_to(rows_ref[0:1, heads], (8, PER_GROUP)), spread_ref[...])
            sent_ref[:, to] = (dot(own_rows, own_in, TN) + near_term * decay[0:1, :]).astype(BF16)


def within_block(
    g, x_ref, dy_ref, b_ref, c_ref, rate_ref, cum_ref, cumt_ref, rows_ref, spread_ref,
    outp_ref, dxp_ref, db_ref, dc_ref, gap_ref, direct_ref, skip_ref, gap_s, direct_s, skip_s,
    rate_s, skips_s,
):
    heads = slice(g * PER_GROUP, (g + 1) * PER_GROUP)
    spreader = spread_ref
    rate_s[...] = over_lanes(rate_ref[:, heads], spreader[...])
    skips_s[...] = over_lanes(jnp.broadcast_to(rows_ref[2:3, heads], (8, PER_GROUP)), spreader[...])
    at_row = lax.broadcasted_iota(jnp.int32, (SPAN, SPAN), 0)
    at_col = lax.broadcasted_iota(jnp.int32, (SPAN, SPAN), 1)
    causal = at_row >= at_col
    first = lax.broadcasted_iota(jnp.int32, (SPAN, PAIR), 1) < P_SIZE
    b_rows, c_rows = b_ref[:, g * N : (g + 1) * N], c_ref[:, g * N : (g + 1) * N]
    scores = jnp.where(causal, dot(c_rows, b_rows, NT), 0.0)
    dscores = jnp.zeros((SPAN, SPAN), F32)
    for j in range(PAIRS):
        lanes = slice(j * PAIR, (j + 1) * PAIR)
        head = g * PER_GROUP + 2 * j
        wide = slice(g * WIDTH + j * PAIR, g * WIDTH + (j + 1) * PAIR)
        x = x_ref[:, wide].astype(F32)
        dy = dy_ref[:, wide]
        rate = rate_s[:, lanes]
        skip = skips_s[0:1, lanes]
        scaled = x * rate
        both = jnp.concatenate(
            [jnp.where(first, scaled, 0.0), jnp.where(first, 0.0, scaled)], axis=0
        ).astype(BF16)
        scaled = scaled.astype(BF16).astype(F32)
        decays = [
            jnp.exp(jnp.minimum(cum_ref[:, h : h + 1] - cumt_ref[h : h + 1, :], 0.0))
            for h in (head, head + 1)
        ]
        mixing = jnp.concatenate([(scores * d).astype(BF16) for d in decays], axis=1)
        intra = dot(mixing, both)
        dmixing = dot(dy, both, NT)
        dscores = dscores + (dmixing[:, :SPAN] * decays[0] + dmixing[:, SPAN:] * decays[1])
        crossed = dot(mixing, dy, TN)
        dscaled = jnp.where(first, crossed[:SPAN], crossed[SPAN:])
        dy = dy.astype(F32)
        direct = scaled * dscaled
        outp_ref[:, lanes] = intra + skip * x
        dxp_ref[:, lanes] = dscaled * rate + skip * dy
        gap_s[:, lanes] = dy * intra - direct
        direct_s[:, lanes] = direct
        skip_s[:, lanes] = jnp.sum((dy * x).reshape(SPAN // 8, 8, PAIR), axis=0)
    dscores = jnp.where(causal, dscores, 0.0).astype(BF16)
    dc_ref[...] = dot(dscores, b_rows)
    db_ref[...] = dot(dscores, c_rows, TN)
    one = spreader[:PER_GROUP, :]
    gap_ref[...] = per_head(gap_s[...], one)
    direct_ref[...] = per_head(direct_s[...], one)
    skip_ref[...] = per_head(skip_s[...], one)


def across_blocks(
    g, place, flag_ref, x_ref, dy_ref, b_ref, c_ref, rate_ref, wide_ref, grow_ref, slope_ref, rows_ref,
    spread_ref, dbp_ref, dcp_ref, gap_ref, direct_ref, skip_ref, outp_ref, dxp_ref, near_ref, crossed_ref,
    passed_ref, *refs,
):
    earlier = refs[:6] if g else ()
    out_ref, dx_ref, db_ref, dc_ref, ddt_ref, par_ref = refs[len(earlier) : len(earlier) + 6]
    out_s, dx_s, rows_s, factor_s, decay_s, gap_s, tail_s, product_s, out_sems, rows_sems = refs[
        len(earlier) + 6 :
    ]
    forward = flag_ref[0] == 1
    inner = flag_ref[1] == 1
    heads = slice(g * PER_GROUP, (g + 1) * PER_GROUP)
    mine = slice(g * N, (g + 1) * N)

    def moves(k):
        lanes = pl.ds(k * TILE, TILE)
        wide = pl.ds(g * WIDTH + k * TILE, TILE)
        pairs = [(out_s.at[:, lanes], out_ref.at[:, wide]), (dx_s.at[:, lanes], dx_ref.at[:, wide])]
        return [pltpu.make_async_copy(a, b, out_sems.at[i, k]) for i, (a, b) in enumerate(pairs)]

    def rows_moves():
        lanes = pl.ds(g * N, N)
        pairs = [(rows_s.at[0], db_ref.at[:, lanes]), (rows_s.at[1], dc_ref.at[:, lanes])]
        return [pltpu.make_async_copy(a, b, rows_sems.at[i]) for i, (a, b) in enumerate(pairs)]

    def work(entering, leaving):
        if entering is not None:
            factor_s[0] = over_lanes(grow_ref[:, heads], spread_ref[...])
        if leaving is not None:
            factor_s[1] = over_lanes(wide_ref[:, heads], spread_ref[...])
        b_rows, c_rows = b_ref[:, mine], c_ref[:, mine]
        db, dc = dbp_ref[...], dcp_ref[...]
        for k in range(WIDTH // TILE):
            lanes = slice(k * TILE, (k + 1) * TILE)
            wide_lanes = slice(g * WIDTH + k * TILE, g * WIDTH + (k + 1) * TILE)
            there = slice(place * WIDTH + k * TILE, place * WIDTH + (k + 1) * TILE)
            out, dx, gap = outp_ref[:, lanes], dxp_ref[:, lanes], 0.0
            if entering is not None:
                enter = entering(lanes, there)
                grow = factor_s[0, :, lanes]
                dy = dy_ref[:, wide_lanes].astype(F32)
                inter = dot(c_rows, enter) * grow
                dc = dc + dot((dy * grow).astype(BF16), enter, NT)
                out = out + inter
                gap = dy * inter
            if leaving is not None:
                leave = leaving(lanes, there)
                wide = factor_s[1, :, lanes]
                dweighted = dot(b_rows, leave)
                weighted = (x_ref[:, wide_lanes].astype(F32) * wide).astype(BF16)
                db = db + dot(weighted, leave, NT)
                dx = dx + wide * dweighted
                tail_term = weighted.astype(F32) * dweighted
                gap = gap - tail_term
                tail_s[:, lanes] = tail_term
            out_s[:, lanes] = out.astype(BF16)
            dx_s[:, lanes] = dx.astype(BF16)
            for move in moves(k):
                move.start()
            gap_s[:, lanes] = gap
            if entering is not None and leaving is not None:
                both = enter.astype(F32) * leave.astype(F32)
                product_s[:, lanes] = jnp.sum(both.reshape(N // 8, 8, TILE), axis=0)
        if leaving is None:
            tail_s[...] = jnp.zeros((SPAN, WIDTH), F32)
        if entering is None or leaving is None:
            product_s[...] = jnp.zeros((8, WIDTH), F32)
        rows_s[0] = db
        rows_s[1] = dc
        for move in rows_moves():
            move.start()

    def near_term(lanes, there):
        return near_ref[:, there]

    def far_term(lanes, there):
        return crossed_ref[:, there]

    def joined(lanes, there):
        decayed = passed_ref[:, there].astype(F32) * decay_s[0:1, lanes]
        return (decayed + near_ref[:, there].astype(F32)).astype(BF16)

    @pl.when(jnp.logical_and(inner, forward))
    def _():
        work(near_term, far_term)

    @pl.when(jnp.logical_and(inner, jnp.logical_not(forward)))
    def _():
        work(far_term, near_term)

    @pl.when(jnp.logical_not(inner))
    def _():
        decay_s[...] = over_lanes(jnp.broadcast_to(rows_ref[3:4, heads], (8, PER_GROUP)), spread_ref[...])

        @pl.when(forward)
        def _():
            work(None, joined)

        @pl.when(jnp.logical_not(forward))
        def _():
            work(joined, None)

    one = spread_ref[:PER_GROUP, :]
    gap = gap_ref[...] + per_head(gap_s[...], one)
    tail_in = per_head(tail_s[...], one)
    product = per_head(product_s[...], one)
    rate = rate_ref[:, heads]
    decay_rate = rows_ref[1:2, heads]
    dtail = jnp.sum(tail_in, axis=0, keepdims=True) + rows_ref[0:1, heads] * jnp.sum(
        product, axis=0, keepdims=True
    )
    at_row = lax.broadcasted_iota(jnp.int32, (SPAN, SPAN), 0)
    at_col = lax.broadcasted_iota(jnp.int32, (SPAN, SPAN), 1)
    upper = jnp.where(at_row <= at_col, 1.0, 0.0)
    dlog = dot(upper, gap, precision=lax.Precision.HIGHEST) + dtail
    drate = (direct_ref[...] + tail_in) / rate - decay_rate * dlog
    ddt = drate * slope_ref[:, heads]
    da = -decay_rate * jnp.sum(rate * dlog, axis=0, keepdims=True)
    dbias = jnp.sum(ddt, axis=0, keepdims=True)
    dskip = jnp.sum(skip_ref[...], axis=0, keepdims=True)
    par = jnp.concatenate([da, dbias, dskip, jnp.zeros((5, PER_GROUP), F32)], axis=0)
    if g == 0:
        ddt_ref[...] = jnp.zeros((SPAN, H), F32)
        par_ref[...] = jnp.zeros((8, H), F32)
    else:
        ddt_ref[...] = earlier[2][...]
        par_ref[...] = earlier[3][...]
    ddt_ref[:, heads] = ddt
    par_ref[:, heads] = par
    for k in range(WIDTH // TILE):
        for move in moves(k):
            move.wait()
    for move in rows_moves():
        move.wait()


SCALARS = pl.BlockSpec(memory_space=pltpu.SMEM)
ANYWHERE = pl.BlockSpec(memory_space=pl.ANY)
PARAMS = pltpu.CompilerParams(vmem_limit_bytes=VMEM_LIMIT)
ON_CHIP = pl.BlockSpec(memory_space=pltpu.VMEM)


def cost(flops, moved):
    return pl.CostEstimate(flops=int(flops), bytes_accessed=int(moved), transcendentals=0)


def call_lay_out():
    return pl.pallas_call(
        lay_out,
        out_specs=ON_CHIP,
        out_shape=jax.ShapeDtypeStruct((2 * PER_GROUP, WIDTH), BF16),
        compiler_params=PARAMS,
        cost_estimate=cost(1, 1),
        name="lay_out",
    )()


def call_prepare(flags, dt_rows, near_dt, params, data):
    square = jax.ShapeDtypeStruct((SPAN, H), F32)
    return pl.pallas_call(
        prepare,
        in_specs=[SCALARS] + [ON_CHIP] * 7,
        out_specs=[ON_CHIP] * 8,
        out_shape=[square] * 7 + [jax.ShapeDtypeStruct((8, H), F32)],
        compiler_params=PARAMS,
        cost_estimate=cost(1, 1),
        name="prepare",
    )(flags, dt_rows, near_dt, params, *data)


def call_pair(groups, start, flags, data, near, prep):
    _, wide, grow, _, _, _, other, rows, spreader = prep
    state = jax.ShapeDtypeStruct((N, len(groups) * WIDTH), BF16)
    return pl.pallas_call(
        functools.partial(pair_state, groups, start),
        in_specs=[SCALARS] + [ON_CHIP] * 11,
        out_specs=[ON_CHIP] * 2,
        out_shape=[state] * 2,
        compiler_params=PARAMS,
        cost_estimate=cost(1, 1),
        name=f"pair{groups[0]}",
    )(flags, *data, *near, wide, grow, other, rows, spreader)


def call_carry(g, flags, data, prep, arrived):
    values, cot, b_rows, c_rows = data
    _, wide, grow, _, _, _, _, rows, spreader = prep
    return pl.pallas_call(
        functools.partial(carry_state, g, bool(arrived)),
        in_specs=[SCALARS] + [ON_CHIP] * (8 + len(arrived)),
        out_specs=ON_CHIP,
        out_shape=jax.ShapeDtypeStruct((N, WIDTH), BF16),
        compiler_params=PARAMS,
        cost_estimate=cost(1, 1),
        name=f"carry{g}",
    )(flags, values, cot, b_rows, c_rows, wide, grow, rows, spreader, *arrived)


def call_within(g, data, prep):
    values, cot, b_rows, c_rows = data
    rate, _, _, cum, cumt, _, _, rows, spreader = prep
    wide_shape = jax.ShapeDtypeStruct((SPAN, WIDTH), F32)
    rows_shape = jax.ShapeDtypeStruct((SPAN, N), F32)
    head_shape = jax.ShapeDtypeStruct((SPAN, PER_GROUP), F32)
    return pl.pallas_call(
        functools.partial(within_block, g),
        in_specs=[ON_CHIP] * 9,
        out_specs=[ON_CHIP] * 7,
        out_shape=[wide_shape] * 2
        + [rows_shape] * 2
        + [head_shape] * 2
        + [jax.ShapeDtypeStruct((8, PER_GROUP), F32)],
        scratch_shapes=[pltpu.VMEM((SPAN, WIDTH), F32)] * 2
        + [pltpu.VMEM((8, WIDTH), F32), pltpu.VMEM((SPAN, WIDTH), F32), pltpu.VMEM((8, WIDTH), F32)],
        compiler_params=PARAMS,
        cost_estimate=cost(1, 1),
        name=f"within{g}",
    )(values, cot, b_rows, c_rows, rate, cum, cumt, rows, spreader)


def call_across(g, place, flags, data, prep, local, states, so_far):
    values, cot, b_rows, c_rows = data
    rate, wide, grow, _, _, slope, _, rows, spreader = prep
    outp, dxp, dbp, dcp, gap, direct, skip = local
    tokens, features = values.shape
    n_in = 21
    if so_far is None:
        earlier, specs, aliases = (), [], {}
    else:
        out, dx, db, dc, ddt, par = so_far
        earlier = (out, dx, ddt, par, db, dc)
        specs = [ANYWHERE, ANYWHERE, ON_CHIP, ON_CHIP, ANYWHERE, ANYWHERE]
        aliases = {n_in: 0, n_in + 1: 1, n_in + 2: 4, n_in + 3: 5, n_in + 4: 2, n_in + 5: 3}
    tiles = WIDTH // TILE
    return pl.pallas_call(
        functools.partial(across_blocks, g, place),
        in_specs=[SCALARS] + [ON_CHIP] * 20 + specs,
        out_specs=[ANYWHERE] * 4 + [ON_CHIP] * 2,
        out_shape=[jax.ShapeDtypeStruct((tokens, features), BF16)] * 2
        + [jax.ShapeDtypeStruct((tokens, G * N), F32)] * 2
        + [jax.ShapeDtypeStruct((tokens, H), F32), jax.ShapeDtypeStruct((8, H), F32)],
        scratch_shapes=[pltpu.VMEM((SPAN, WIDTH), BF16)] * 2
        + [pltpu.VMEM((2, SPAN, N), F32), pltpu.VMEM((2, SPAN, WIDTH), F32), pltpu.VMEM((8, WIDTH), F32)]
        + [pltpu.VMEM((SPAN, WIDTH), F32)] * 2
        + [pltpu.VMEM((8, WIDTH), F32)]
        + [pltpu.SemaphoreType.DMA((2, tiles)), pltpu.SemaphoreType.DMA((2,))],
        input_output_aliases=aliases,
        compiler_params=PARAMS,
        cost_estimate=cost(1, 1),
        name=f"across{g}",
    )(flags, values, cot, b_rows, c_rows, rate, wide, grow, slope, rows, spreader,
      dbp, dcp, gap, direct, skip, outp, dxp, *states, *earlier)


def per_device(values, b_rows, c_rows, dt_rows, a_log, dt_bias, d_skip, cotangent):
    ranks = lax.axis_size("seq")
    copies = lax.axis_size("dp")
    rank = lax.axis_index("seq")
    tokens = values.shape[1]
    mine = a_log.shape[0]
    data = (
        values.reshape(tokens, H * P_SIZE),
        cotangent.reshape(tokens, H * P_SIZE),
        b_rows.reshape(tokens, G * N),
        c_rows.reshape(tokens, G * N),
    )
    own = jnp.concatenate([jnp.stack([a_log, dt_bias, d_skip]), jnp.zeros((5, mine), F32)], axis=0)
    at_lane = lax.broadcasted_iota(jnp.int32, (8, H), 1) // mine
    own = jnp.where(at_lane == rank, jnp.tile(own, (1, ranks)), 0.0)
    own_dt = dt_rows.reshape(tokens, H)
    half = ranks // 2
    forward = rank < half
    depth = jnp.where(forward, rank, ranks - 1 - rank)

    def flags(*bits):
        return jnp.stack([jnp.asarray(bit) for bit in bits]).astype(jnp.int32)

    def both_ways(step):
        return [(step, step + 1), (ranks - 1 - step, ranks - 2 - step)]

    if ranks == 4:
        marks = flags(forward, depth == 1, rank % 2 == 1)
        swap = [(i, i ^ 1) for i in range(ranks)]
        def after(value, *others):
            return lax.optimization_barrier((value, *others))[0]

        mine_dt = jnp.concatenate([own_dt, own], axis=0)
        near_dt = lax.ppermute(mine_dt, "seq", swap)
        even = rank % 2 == 0
        near_rows = lax.ppermute(jnp.where(even, data[2], data[3]), "seq", swap)

        def from_near(first, last, x, dy):
            lanes = slice(first * WIDTH, last * WIDTH)
            return lax.ppermute(jnp.where(even, x[:, lanes], dy[:, lanes]), "seq", swap)

        parts = ((0,), (1, 2), (3,))
        near = from_near(0, 1, data[0], data[1])
        params = own + near_dt[SPAN:]
        params = params + lax.ppermute(params, "seq", [(i, i ^ 2) for i in range(ranks)])
        prep = (*call_prepare(marks, own_dt, near_dt, params, data), call_lay_out())

        def prep_after(token):
            return (*prep[:7], after(prep[7], token), prep[8])

        pairs = [call_pair(parts[0], 0, marks, data, (near, near_rows), prep)]
        rest, _ = lax.optimization_barrier((data[:2], pairs[0][0]))
        near = from_near(1, G, *rest)
        local = [call_within(0, data, prep_after(pairs[0][0]))]
        for part in parts[1:]:
            ready = prep_after(local[0][-1] if len(pairs) == 1 else pairs[-1][0])
            pairs.append(call_pair(part, 1, marks, data, (near, near_rows), ready))
        crossed = [lax.ppermute(sent, "seq", both_ways(1)) for _, sent in pairs]
        token = pairs[-1][0]
        for g in range(1, G):
            local.append(call_within(g, data, prep_after(token)))
            token = local[g][-1]

        def pass_on(k, *tokens):
            arrived = after(crossed[k], *tokens)
            return arrived, lax.ppermute(arrived, "seq", both_ways(2))

        states = (pairs[0][0], *pass_on(0, local[1][-1]))
        result = call_across(0, 0, marks, data, prep, local[0], states, None)
        states = (pairs[1][0], *pass_on(1, local[3][-1], result[-1]))
        result = call_across(1, 0, marks, data, prep, local[1], states, result)
        result = call_across(2, 1, marks, data, prep, local[2], states, result)
        last = (pairs[2][0], *pass_on(2, result[-1]))
        result = call_across(3, 0, marks, data, prep, local[3], last, result)
    else:
        marks = flags(forward, True, True)
        params = lax.psum(own, "seq")
        prep = (*call_prepare(marks, own_dt, own_dt, params, data), call_lay_out())
        states = []
        for g in range(G):
            first = None
            for step in range(half):
                arrived = () if first is None else (first,)
                sent = call_carry(g, flags(forward, depth == step), data, prep, arrived)
                got = lax.ppermute(sent, "seq", both_ways(step))
                if step < half - 1:
                    first = got if first is None else first + got
            for step in range(half, ranks - 1):
                role = flags(jnp.logical_not(forward), depth == ranks - 1 - step)
                sent = call_carry(g, role, data, prep, (got,))
                got = got + lax.ppermute(sent, "seq", both_ways(step))
            states.append((jnp.zeros_like(got) if first is None else first, got, got))
        result = None
        for g in range(G):
            local = call_within(g, data, prep)
            result = call_across(g, 0, marks, data, prep, local, states[g], result)
    out, dx, db, dc, ddt, par = result
    for axis, size in (("seq", ranks), ("dp", copies)):
        hop = 1
        while hop < size:
            def swapped(bits):
                return lax.ppermute(par, axis, [(i, i ^ bits) for i in range(size)])

            if 2 * hop < size:
                par = (par + swapped(hop)) + (swapped(2 * hop) + swapped(3 * hop))
            else:
                par = par + swapped(hop)
            hop *= 4
    grad_params = lax.dynamic_slice_in_dim(par, rank * mine, mine, 1)[:3]
    return (
        out.reshape(1, tokens, H * P_SIZE),
        dx.reshape(1, tokens, H * P_SIZE),
        db.reshape(1, tokens, G * N),
        dc.reshape(1, tokens, G * N),
        ddt.reshape(1, tokens, H),
        grad_params,
    )


def solution(mesh):
    rows = P("dp", "seq", None)
    heads = P("seq")
    return jax.shard_map(
        per_device,
        mesh=mesh,
        in_specs=(rows, rows, rows, rows, heads, heads, heads, rows),
        out_specs=(rows, rows, rows, rows, rows, P(None, "seq")),
        check_vma=False,
    )
```

```python
import functools

import jax
import jax.numpy as jnp
from jax import lax
from jax.experimental import pallas as pl
from jax.experimental.pallas import tpu as pltpu
from jax.sharding import PartitionSpec as P

H = 128
G = 4
P_SIZE = 64
N = 256
SPAN = 128
PER_GROUP = H // G
WIDTH = PER_GROUP * P_SIZE
PAIR = 2 * P_SIZE
PAIRS = PER_GROUP // 2
TILE = 512
VMEM_LIMIT = 24 * 1024 * 1024

F32 = jnp.float32
BF16 = jnp.bfloat16
NN = (((1,), (0,)), ((), ()))
NT = (((1,), (1,)), ((), ()))
TN = (((0,), (0,)), ((), ()))


def dot(left, right, dims=NN, precision=None):
    return lax.dot_general(left, right, dims, precision=precision, preferred_element_type=F32)


def split(a):
    high = a.astype(BF16)
    low = (a - high.astype(F32)).astype(BF16)
    return jnp.concatenate([high, low], axis=1)


def spread(rows, width):
    head = lax.broadcasted_iota(jnp.int32, (rows, width), 0) & (PER_GROUP - 1)
    lane = lax.broadcasted_iota(jnp.int32, (rows, width), 1) >> 6
    return jnp.where(head == lane, 1.0, 0.0).astype(BF16)


def over_lanes(a, spreader):
    return dot(split(a), spreader)


def per_head(a, spreader):
    high = a.astype(BF16)
    low = (a - high.astype(F32)).astype(BF16)
    return dot(high, spreader, NT) + dot(low, spreader, NT)


def decays(raw, decay_rate):
    rate = jnp.maximum(raw, 0.0) + jnp.log1p(jnp.exp(-jnp.abs(raw)))
    at_row = lax.broadcasted_iota(jnp.int32, (SPAN, SPAN), 0)
    at_col = lax.broadcasted_iota(jnp.int32, (SPAN, SPAN), 1)
    lower = jnp.where(at_row >= at_col, 1.0, 0.0)
    cum = dot(lower, -rate * decay_rate, precision=lax.Precision.HIGHEST)
    tail = cum[SPAN - 1 : SPAN, :]
    wide = jnp.exp(jnp.minimum(tail - cum, 0.0)) * rate
    return rate, cum, tail, wide, jnp.exp(cum)


def lay_out(spread_ref):
    spread_ref[...] = spread(2 * PER_GROUP, WIDTH)


def prepare(flag_ref, dt_ref, near_ref, param_ref, *refs):
    rate_ref, wide_ref, grow_ref, cum_ref, cumt_ref, slope_ref, other_ref, rows_ref = refs[-8:]
    params = param_ref[...]
    decay_rate = jnp.exp(params[0:1, :])
    raw = dt_ref[...] + params[1:2, :]
    rate, cum, tail, wide, grow = decays(raw, decay_rate)
    rate_ref[...] = rate
    wide_ref[...] = wide
    grow_ref[...] = grow
    cum_ref[...] = cum
    cumt_ref[...] = cum.T
    small = jnp.exp(-jnp.abs(raw))
    slope_ref[...] = jnp.where(raw >= 0.0, 1.0, small) / (1.0 + small)
    _, _, near_tail, near_wide, near_grow = decays(near_ref[:SPAN, :] + params[1:2, :], decay_rate)
    other_ref[...] = jnp.where(flag_ref[2] == 1, near_wide, near_grow)
    rows_ref[...] = jnp.concatenate(
        [jnp.exp(tail), decay_rate, params[2:3, :], jnp.exp(near_tail), jnp.zeros((4, H), F32)], axis=0
    )


def carry_state(
    g, carried, flag_ref, x_ref, dy_ref, b_ref, c_ref, wide_ref, grow_ref, rows_ref, spread_ref, *refs
):
    sent_ref = refs[-1]

    @pl.when(flag_ref[1] == 1)
    def _():
        forward = flag_ref[0] == 1
        heads = slice(g * PER_GROUP, (g + 1) * PER_GROUP)
        factor = jnp.where(forward, wide_ref[:, heads], grow_ref[:, heads])
        own_rows = jnp.where(
            forward, b_ref[:, g * N : (g + 1) * N], c_ref[:, g * N : (g + 1) * N]
        )
        spreader = spread_ref
        factor_hl = split(factor)
        decay_hl = split(jnp.broadcast_to(rows_ref[0:1, heads], (8, PER_GROUP)))
        for lo in range(0, WIDTH, TILE):
            lanes = slice(lo, lo + TILE)
            wide = slice(g * WIDTH + lo, g * WIDTH + lo + TILE)
            inputs = jnp.where(forward, x_ref[:, wide], dy_ref[:, wide]).astype(F32)
            weighted = (inputs * dot(factor_hl, spreader[:, lanes])).astype(BF16)
            state = dot(own_rows, weighted, TN)
            if carried:
                arrived = refs[0][:, lanes].astype(F32)
                for more in refs[1:-1]:
                    arrived = arrived + more[:, lanes].astype(F32)
                decay = dot(decay_hl, spreader[:, lanes])[0:1, :]
                state = state + arrived * decay
            sent_ref[:, lanes] = state.astype(BF16)


def pair_state(
    groups, start, flag_ref, x_ref, dy_ref, b_ref, c_ref, near_in_ref, near_rows_ref, wide_ref, grow_ref,
    other_ref, rows_ref, spread_ref, near_ref, sent_ref,
):
    onward = flag_ref[2] == 1
    for k, g in enumerate(groups):
        heads = slice(g * PER_GROUP, (g + 1) * PER_GROUP)
        rows = slice(g * N, (g + 1) * N)
        wide = slice(g * WIDTH, (g + 1) * WIDTH)
        to = slice(k * WIDTH, (k + 1) * WIDTH)
        near_in = near_in_ref[:, (g - start) * WIDTH : (g - start + 1) * WIDTH].astype(F32) * over_lanes(other_ref[:, heads], spread_ref[...])
        near_term = dot(near_rows_ref[:, rows], near_in.astype(BF16), TN)
        near_ref[:, to] = near_term.astype(BF16)

        @pl.when(flag_ref[1] == 1)
        def _(near_term=near_term, heads=heads, rows=rows, wide=wide, to=to):
            own_rows = jnp.where(onward, b_ref[:, rows], c_ref[:, rows])
            own_in = jnp.where(onward, x_ref[:, wide], dy_ref[:, wide]).astype(F32)
            factor = jnp.where(onward, wide_ref[:, heads], grow_ref[:, heads])
            own_in = (own_in * over_lanes(factor, spread_ref[...])).astype(BF16)
            decay = over_lanes(jnp.broadcast_to(rows_ref[0:1, heads], (8, PER_GROUP)), spread_ref[...])
            sent_ref[:, to] = (dot(own_rows, own_in, TN) + near_term * decay[0:1, :]).astype(BF16)


def within_block(
    g, x_ref, dy_ref, b_ref, c_ref, rate_ref, cum_ref, cumt_ref, rows_ref, spread_ref,
    outp_ref, dxp_ref, db_ref, dc_ref, gap_ref, direct_ref, skip_ref, gap_s, direct_s, skip_s,
    rate_s, skips_s,
):
    heads = slice(g * PER_GROUP, (g + 1) * PER_GROUP)
    spreader = spread_ref
    rate_s[...] = over_lanes(rate_ref[:, heads], spreader[...])
    skips_s[...] = over_lanes(jnp.broadcast_to(rows_ref[2:3, heads], (8, PER_GROUP)), spreader[...])
    at_row = lax.broadcasted_iota(jnp.int32, (SPAN, SPAN), 0)
    at_col = lax.broadcasted_iota(jnp.int32, (SPAN, SPAN), 1)
    causal = at_row >= at_col
    first = lax.broadcasted_iota(jnp.int32, (SPAN, PAIR), 1) < P_SIZE
    b_rows, c_rows = b_ref[:, g * N : (g + 1) * N], c_ref[:, g * N : (g + 1) * N]
    scores = jnp.where(causal, dot(c_rows, b_rows, NT), 0.0)
    dscores = jnp.zeros((SPAN, SPAN), F32)
    for j in range(PAIRS):
        lanes = slice(j * PAIR, (j + 1) * PAIR)
        head = g * PER_GROUP + 2 * j
        wide = slice(g * WIDTH + j * PAIR, g * WIDTH + (j + 1) * PAIR)
        x = x_ref[:, wide].astype(F32)
        dy = dy_ref[:, wide]
        rate = rate_s[:, lanes]
        skip = skips_s[0:1, lanes]
        scaled = x * rate
        both = jnp.concatenate(
            [jnp.where(first, scaled, 0.0), jnp.where(first, 0.0, scaled)], axis=0
        ).astype(BF16)
        scaled = scaled.astype(BF16).astype(F32)
        decays = [
            jnp.exp(jnp.minimum(cum_ref[:, h : h + 1] - cumt_ref[h : h + 1, :], 0.0))
            for h in (head, head + 1)
        ]
        mixing = jnp.concatenate([(scores * d).astype(BF16) for d in decays], axis=1)
        intra = dot(mixing, both)
        dmixing = dot(dy, both, NT)
        dscores = dscores + (dmixing[:, :SPAN] * decays[0] + dmixing[:, SPAN:] * decays[1])
        crossed = dot(mixing, dy, TN)
        dscaled = jnp.where(first, crossed[:SPAN], crossed[SPAN:])
        dy = dy.astype(F32)
        direct = scaled * dscaled
        outp_ref[:, lanes] = intra + skip * x
        dxp_ref[:, lanes] = dscaled * rate + skip * dy
        gap_s[:, lanes] = dy * intra - direct
        direct_s[:, lanes] = direct
        skip_s[:, lanes] = jnp.sum((dy * x).reshape(SPAN // 8, 8, PAIR), axis=0)
    dscores = jnp.where(causal, dscores, 0.0).astype(BF16)
    dc_ref[...] = dot(dscores, b_rows)
    db_ref[...] = dot(dscores, c_rows, TN)
    one = spreader[:PER_GROUP, :]
    gap_ref[...] = per_head(gap_s[...], one)
    direct_ref[...] = per_head(direct_s[...], one)
    skip_ref[...] = per_head(skip_s[...], one)


def across_blocks(
    g, place, flag_ref, x_ref, dy_ref, b_ref, c_ref, rate_ref, wide_ref, grow_ref, slope_ref, rows_ref,
    spread_ref, dbp_ref, dcp_ref, gap_ref, direct_ref, skip_ref, outp_ref, dxp_ref, near_ref, crossed_ref,
    passed_ref, *refs,
):
    last = g == G - 1
    earlier = [refs[6 * i : 6 * i + 6] for i in range(g)] if last else []
    refs = refs[6 * len(earlier) :]
    out_ref, dx_ref, db_ref, dc_ref, ddt_ref, par_ref = refs[:6]
    factor_s, decay_s, gap_s, tail_s, product_s, *more = refs[6:]
    if last:
        out_s, dx_s, rows_s, sems = more
    else:
        out_s, dx_s = out_ref, dx_ref
    forward = flag_ref[0] == 1
    inner = flag_ref[1] == 1
    heads = slice(g * PER_GROUP, (g + 1) * PER_GROUP)
    mine = slice(g * N, (g + 1) * N)

    def moves(of):
        wide, rows = pl.ds(of * WIDTH, WIDTH), pl.ds(of * N, N)
        out, dx, db, dc = (out_s, dx_s, rows_s.at[0], rows_s.at[1]) if of == g else earlier[of][:4]
        pairs = [
            (out, out_ref.at[:, wide]),
            (dx, dx_ref.at[:, wide]),
            (db, db_ref.at[:, rows]),
            (dc, dc_ref.at[:, rows]),
        ]
        return [pltpu.make_async_copy(a, b, sems.at[of, i]) for i, (a, b) in enumerate(pairs)]

    if last:
        for of in range(g):
            for move in moves(of):
                move.start()

    def work(entering, leaving):
        if entering is not None:
            factor_s[0] = over_lanes(grow_ref[:, heads], spread_ref[...])
        if leaving is not None:
            factor_s[1] = over_lanes(wide_ref[:, heads], spread_ref[...])
        b_rows, c_rows = b_ref[:, mine], c_ref[:, mine]
        db, dc = dbp_ref[...], dcp_ref[...]
        for k in range(WIDTH // TILE):
            lanes = slice(k * TILE, (k + 1) * TILE)
            wide_lanes = slice(g * WIDTH + k * TILE, g * WIDTH + (k + 1) * TILE)
            there = slice(place * WIDTH + k * TILE, place * WIDTH + (k + 1) * TILE)
            out, dx, gap = outp_ref[:, lanes], dxp_ref[:, lanes], 0.0
            if entering is not None:
                enter = entering(lanes, there)
                grow = factor_s[0, :, lanes]
                dy = dy_ref[:, wide_lanes].astype(F32)
                inter = dot(c_rows, enter) * grow
                dc = dc + dot((dy * grow).astype(BF16), enter, NT)
                out = out + inter
                gap = dy * inter
            if leaving is not None:
                leave = leaving(lanes, there)
                wide = factor_s[1, :, lanes]
                dweighted = dot(b_rows, leave)
                weighted = (x_ref[:, wide_lanes].astype(F32) * wide).astype(BF16)
                db = db + dot(weighted, leave, NT)
                dx = dx + wide * dweighted
                tail_term = weighted.astype(F32) * dweighted
                gap = gap - tail_term
                tail_s[:, lanes] = tail_term
            out_s[:, lanes] = out.astype(BF16)
            dx_s[:, lanes] = dx.astype(BF16)
            gap_s[:, lanes] = gap
            if entering is not None and leaving is not None:
                both = enter.astype(F32) * leave.astype(F32)
                product_s[:, lanes] = jnp.sum(both.reshape(N // 8, 8, TILE), axis=0)
        if leaving is None:
            tail_s[...] = jnp.zeros((SPAN, WIDTH), F32)
        if entering is None or leaving is None:
            product_s[...] = jnp.zeros((8, WIDTH), F32)
        if last:
            rows_s[0] = db
            rows_s[1] = dc
        else:
            db_ref[...] = db
            dc_ref[...] = dc

    def near_term(lanes, there):
        return near_ref[:, there]

    def far_term(lanes, there):
        return crossed_ref[:, there]

    def joined(lanes, there):
        decayed = passed_ref[:, there].astype(F32) * decay_s[0:1, lanes]
        return (decayed + near_ref[:, there].astype(F32)).astype(BF16)

    @pl.when(jnp.logical_and(inner, forward))
    def _():
        work(near_term, far_term)

    @pl.when(jnp.logical_and(inner, jnp.logical_not(forward)))
    def _():
        work(far_term, near_term)

    @pl.when(jnp.logical_not(inner))
    def _():
        decay_s[...] = over_lanes(jnp.broadcast_to(rows_ref[3:4, heads], (8, PER_GROUP)), spread_ref[...])

        @pl.when(forward)
        def _():
            work(None, joined)

        @pl.when(jnp.logical_not(forward))
        def _():
            work(joined, None)

    if last:
        for move in moves(g):
            move.start()
    one = spread_ref[:PER_GROUP, :]
    gap = gap_ref[...] + per_head(gap_s[...], one)
    tail_in = per_head(tail_s[...], one)
    product = per_head(product_s[...], one)
    rate = rate_ref[:, heads]
    decay_rate = rows_ref[1:2, heads]
    dtail = jnp.sum(tail_in, axis=0, keepdims=True) + rows_ref[0:1, heads] * jnp.sum(
        product, axis=0, keepdims=True
    )
    at_row = lax.broadcasted_iota(jnp.int32, (SPAN, SPAN), 0)
    at_col = lax.broadcasted_iota(jnp.int32, (SPAN, SPAN), 1)
    upper = jnp.where(at_row <= at_col, 1.0, 0.0)
    dlog = dot(upper, gap, precision=lax.Precision.HIGHEST) + dtail
    drate = (direct_ref[...] + tail_in) / rate - decay_rate * dlog
    ddt = drate * slope_ref[:, heads]
    da = -decay_rate * jnp.sum(rate * dlog, axis=0, keepdims=True)
    dbias = jnp.sum(ddt, axis=0, keepdims=True)
    dskip = jnp.sum(skip_ref[...], axis=0, keepdims=True)
    par = jnp.concatenate([da, dbias, dskip, jnp.zeros((5, PER_GROUP), F32)], axis=0)
    if last:
        ddt_ref[...] = jnp.concatenate([before[4][...] for before in earlier] + [ddt], axis=1)
        par_ref[...] = jnp.concatenate([before[5][...] for before in earlier] + [par], axis=1)
        for of in range(G):
            for move in moves(of):
                move.wait()
    else:
        ddt_ref[...] = ddt
        par_ref[...] = par


SCALARS = pl.BlockSpec(memory_space=pltpu.SMEM)
ANYWHERE = pl.BlockSpec(memory_space=pl.ANY)
PARAMS = pltpu.CompilerParams(vmem_limit_bytes=VMEM_LIMIT)
ON_CHIP = pl.BlockSpec(memory_space=pltpu.VMEM)


def cost(flops, moved):
    return pl.CostEstimate(flops=int(flops), bytes_accessed=int(moved), transcendentals=0)


def call_lay_out():
    return pl.pallas_call(
        lay_out,
        out_specs=ON_CHIP,
        out_shape=jax.ShapeDtypeStruct((2 * PER_GROUP, WIDTH), BF16),
        compiler_params=PARAMS,
        cost_estimate=cost(1, 1),
        name="lay_out",
    )()


def call_prepare(flags, dt_rows, near_dt, params, data):
    square = jax.ShapeDtypeStruct((SPAN, H), F32)
    return pl.pallas_call(
        prepare,
        in_specs=[SCALARS] + [ON_CHIP] * 7,
        out_specs=[ON_CHIP] * 8,
        out_shape=[square] * 7 + [jax.ShapeDtypeStruct((8, H), F32)],
        compiler_params=PARAMS,
        cost_estimate=cost(1, 1),
        name="prepare",
    )(flags, dt_rows, near_dt, params, *data)


def call_pair(groups, start, flags, data, near, prep):
    _, wide, grow, _, _, _, other, rows, spreader = prep
    state = jax.ShapeDtypeStruct((N, len(groups) * WIDTH), BF16)
    return pl.pallas_call(
        functools.partial(pair_state, groups, start),
        in_specs=[SCALARS] + [ON_CHIP] * 11,
        out_specs=[ON_CHIP] * 2,
        out_shape=[state] * 2,
        compiler_params=PARAMS,
        cost_estimate=cost(1, 1),
        name=f"pair{groups[0]}",
    )(flags, *data, *near, wide, grow, other, rows, spreader)


def call_carry(g, flags, data, prep, arrived):
    values, cot, b_rows, c_rows = data
    _, wide, grow, _, _, _, _, rows, spreader = prep
    return pl.pallas_call(
        functools.partial(carry_state, g, bool(arrived)),
        in_specs=[SCALARS] + [ON_CHIP] * (8 + len(arrived)),
        out_specs=ON_CHIP,
        out_shape=jax.ShapeDtypeStruct((N, WIDTH), BF16),
        compiler_params=PARAMS,
        cost_estimate=cost(1, 1),
        name=f"carry{g}",
    )(flags, values, cot, b_rows, c_rows, wide, grow, rows, spreader, *arrived)


def call_within(g, data, prep):
    values, cot, b_rows, c_rows = data
    rate, _, _, cum, cumt, _, _, rows, spreader = prep
    wide_shape = jax.ShapeDtypeStruct((SPAN, WIDTH), F32)
    rows_shape = jax.ShapeDtypeStruct((SPAN, N), F32)
    head_shape = jax.ShapeDtypeStruct((SPAN, PER_GROUP), F32)
    return pl.pallas_call(
        functools.partial(within_block, g),
        in_specs=[ON_CHIP] * 9,
        out_specs=[ON_CHIP] * 7,
        out_shape=[wide_shape] * 2
        + [rows_shape] * 2
        + [head_shape] * 2
        + [jax.ShapeDtypeStruct((8, PER_GROUP), F32)],
        scratch_shapes=[pltpu.VMEM((SPAN, WIDTH), F32)] * 2
        + [pltpu.VMEM((8, WIDTH), F32), pltpu.VMEM((SPAN, WIDTH), F32), pltpu.VMEM((8, WIDTH), F32)],
        compiler_params=PARAMS,
        cost_estimate=cost(1, 1),
        name=f"within{g}",
    )(values, cot, b_rows, c_rows, rate, cum, cumt, rows, spreader)


def call_across(g, place, flags, data, prep, local, states, earlier):
    values, cot, b_rows, c_rows = data
    rate, wide, grow, _, _, slope, _, rows, spreader = prep
    outp, dxp, dbp, dcp, gap, direct, skip = local
    last = g == G - 1
    groups = G if last else 1
    tokens = values.shape[0]
    before = [a for result in earlier for a in result] if last else []
    scratch = [pltpu.VMEM((2, SPAN, WIDTH), F32), pltpu.VMEM((8, WIDTH), F32)]
    scratch += [pltpu.VMEM((SPAN, WIDTH), F32)] * 2 + [pltpu.VMEM((8, WIDTH), F32)]
    if last:
        scratch += [pltpu.VMEM((SPAN, WIDTH), BF16)] * 2
        scratch += [pltpu.VMEM((2, SPAN, N), F32), pltpu.SemaphoreType.DMA((G, 4))]
    return pl.pallas_call(
        functools.partial(across_blocks, g, place),
        in_specs=[SCALARS] + [ON_CHIP] * (20 + len(before)),
        out_specs=[ANYWHERE if last else ON_CHIP] * 4 + [ON_CHIP] * 2,
        out_shape=[jax.ShapeDtypeStruct((tokens, groups * WIDTH), BF16)] * 2
        + [jax.ShapeDtypeStruct((tokens, groups * N), F32)] * 2
        + [jax.ShapeDtypeStruct((rows_, groups * PER_GROUP), F32) for rows_ in (tokens, 8)],
        scratch_shapes=scratch,
        compiler_params=PARAMS,
        cost_estimate=cost(1, 1),
        name=f"across{g}",
    )(flags, values, cot, b_rows, c_rows, rate, wide, grow, slope, rows, spreader,
      dbp, dcp, gap, direct, skip, outp, dxp, *states, *before)


def per_device(values, b_rows, c_rows, dt_rows, a_log, dt_bias, d_skip, cotangent):
    ranks = lax.axis_size("seq")
    copies = lax.axis_size("dp")
    rank = lax.axis_index("seq")
    tokens = values.shape[1]
    mine = a_log.shape[0]
    data = (
        values.reshape(tokens, H * P_SIZE),
        cotangent.reshape(tokens, H * P_SIZE),
        b_rows.reshape(tokens, G * N),
        c_rows.reshape(tokens, G * N),
    )
    own = jnp.concatenate([jnp.stack([a_log, dt_bias, d_skip]), jnp.zeros((5, mine), F32)], axis=0)
    at_lane = lax.broadcasted_iota(jnp.int32, (8, H), 1) // mine
    own = jnp.where(at_lane == rank, jnp.tile(own, (1, ranks)), 0.0)
    own_dt = dt_rows.reshape(tokens, H)
    half = ranks // 2
    forward = rank < half
    depth = jnp.where(forward, rank, ranks - 1 - rank)

    def flags(*bits):
        return jnp.stack([jnp.asarray(bit) for bit in bits]).astype(jnp.int32)

    def both_ways(step):
        return [(step, step + 1), (ranks - 1 - step, ranks - 2 - step)]

    if ranks == 4:
        marks = flags(forward, depth == 1, rank % 2 == 1)
        swap = [(i, i ^ 1) for i in range(ranks)]
        def after(value, *others):
            return lax.optimization_barrier((value, *others))[0]

        mine_dt = jnp.concatenate([own_dt, own], axis=0)
        near_dt = lax.ppermute(mine_dt, "seq", swap)
        even = rank % 2 == 0
        near_rows = lax.ppermute(jnp.where(even, data[2], data[3]), "seq", swap)

        def from_near(first, last, x, dy):
            lanes = slice(first * WIDTH, last * WIDTH)
            return lax.ppermute(jnp.where(even, x[:, lanes], dy[:, lanes]), "seq", swap)

        parts = ((0,), (1, 2), (3,))
        near = from_near(0, 1, data[0], data[1])
        params = own + near_dt[SPAN:]
        params = params + lax.ppermute(params, "seq", [(i, i ^ 2) for i in range(ranks)])
        prep = (*call_prepare(marks, own_dt, near_dt, params, data), call_lay_out())

        def prep_after(token):
            return (*prep[:7], after(prep[7], token), prep[8])

        pairs = [call_pair(parts[0], 0, marks, data, (near, near_rows), prep)]
        rest, _ = lax.optimization_barrier((data[:2], pairs[0][0]))
        near = from_near(1, G, *rest)
        local = [call_within(0, data, prep_after(pairs[0][0]))]
        for part in parts[1:]:
            ready = prep_after(local[0][-1] if len(pairs) == 1 else pairs[-1][0])
            pairs.append(call_pair(part, 1, marks, data, (near, near_rows), ready))
        crossed = [lax.ppermute(sent, "seq", both_ways(1)) for _, sent in pairs]
        token = pairs[-1][0]
        for g in range(1, G - 1):
            local.append(call_within(g, data, prep_after(token)))
            token = local[g][-1]

        def pass_on(k, *tokens):
            arrived = after(crossed[k], *tokens)
            return arrived, lax.ppermute(arrived, "seq", both_ways(2))

        def finish(g, place, states, earlier):
            ready = prep_after(local[-1][-1])
            if earlier:
                ready = (*ready[:7], after(ready[7], earlier[-1][-1]), ready[8])
            return (*earlier, call_across(g, place, marks, data, ready, local[g], states, earlier))

        states = (pairs[0][0], *pass_on(0, local[1][-1]))
        results = finish(0, 0, states, ())
        states = (pairs[1][0], *pass_on(1, local[2][-1], results[-1][-1]))
        local.append(call_within(3, data, prep_after(states[1])))
        results = finish(1, 0, states, results)
        final = (pairs[2][0], *pass_on(2, results[-1][-1]))
        results = finish(2, 1, states, results)
        result = finish(3, 0, final, results)[-1]
    else:
        marks = flags(forward, True, True)
        params = lax.psum(own, "seq")
        prep = (*call_prepare(marks, own_dt, own_dt, params, data), call_lay_out())
        states = []
        for g in range(G):
            first = None
            for step in range(half):
                arrived = () if first is None else (first,)
                sent = call_carry(g, flags(forward, depth == step), data, prep, arrived)
                got = lax.ppermute(sent, "seq", both_ways(step))
                if step < half - 1:
                    first = got if first is None else first + got
            for step in range(half, ranks - 1):
                role = flags(jnp.logical_not(forward), depth == ranks - 1 - step)
                sent = call_carry(g, role, data, prep, (got,))
                got = got + lax.ppermute(sent, "seq", both_ways(step))
            states.append((jnp.zeros_like(got) if first is None else first, got, got))
        results = ()
        for g in range(G):
            local = call_within(g, data, prep)
            results += (call_across(g, 0, marks, data, prep, local, states[g], results),)
        result = results[-1]

    out, dx, db, dc, ddt, par = result
    for axis, size in (("seq", ranks), ("dp", copies)):
        hop = 1
        while hop < size:
            def swapped(bits):
                return lax.ppermute(par, axis, [(i, i ^ bits) for i in range(size)])

            if 2 * hop < size:
                par = (par + swapped(hop)) + (swapped(2 * hop) + swapped(3 * hop))
            else:
                par = par + swapped(hop)
            hop *= 4
    grad_params = lax.dynamic_slice_in_dim(par, rank * mine, mine, 1)[:3]
    return (
        out.reshape(1, tokens, H * P_SIZE),
        dx.reshape(1, tokens, H * P_SIZE),
        db.reshape(1, tokens, G * N),
        dc.reshape(1, tokens, G * N),
        ddt.reshape(1, tokens, H),
        grad_params,
    )


def solution(mesh):
    rows = P("dp", "seq", None)
    heads = P("seq")
    return jax.shard_map(
        per_device,
        mesh=mesh,
        in_specs=(rows, rows, rows, rows, heads, heads, heads, rows),
        out_specs=(rows, rows, rows, rows, rows, P(None, "seq")),
        check_vma=False,
    )
```

```python
import functools

import jax
import jax.numpy as jnp
from jax import lax
from jax.experimental import pallas as pl
from jax.experimental.pallas import tpu as pltpu
from jax.sharding import PartitionSpec as P

H = 128
G = 4
P_SIZE = 64
N = 256
SPAN = 128
PER_GROUP = H // G
WIDTH = PER_GROUP * P_SIZE
PAIR = 2 * P_SIZE
PAIRS = PER_GROUP // 2
TILE = 512
VMEM_LIMIT = 24 * 1024 * 1024

F32 = jnp.float32
BF16 = jnp.bfloat16
NN = (((1,), (0,)), ((), ()))
NT = (((1,), (1,)), ((), ()))
TN = (((0,), (0,)), ((), ()))


def dot(left, right, dims=NN, precision=None):
    return lax.dot_general(left, right, dims, precision=precision, preferred_element_type=F32)


def split(a):
    high = a.astype(BF16)
    low = (a - high.astype(F32)).astype(BF16)
    return jnp.concatenate([high, low], axis=1)


def spread(rows, width):
    head = lax.broadcasted_iota(jnp.int32, (rows, width), 0) & (PER_GROUP - 1)
    lane = lax.broadcasted_iota(jnp.int32, (rows, width), 1) >> 6
    return jnp.where(head == lane, 1.0, 0.0).astype(BF16)


def over_lanes(a, spreader):
    return dot(split(a), spreader)


def per_head(a, spreader):
    high = a.astype(BF16)
    low = (a - high.astype(F32)).astype(BF16)
    return dot(high, spreader, NT) + dot(low, spreader, NT)


def decays(raw, decay_rate):
    rate = jnp.maximum(raw, 0.0) + jnp.log1p(jnp.exp(-jnp.abs(raw)))
    at_row = lax.broadcasted_iota(jnp.int32, (SPAN, SPAN), 0)
    at_col = lax.broadcasted_iota(jnp.int32, (SPAN, SPAN), 1)
    lower = jnp.where(at_row >= at_col, 1.0, 0.0)
    cum = dot(lower, -rate * decay_rate, precision=lax.Precision.HIGHEST)
    tail = cum[SPAN - 1 : SPAN, :]
    wide = jnp.exp(jnp.minimum(tail - cum, 0.0)) * rate
    return rate, cum, tail, wide, jnp.exp(cum)


def lay_out(spread_ref):
    spread_ref[...] = spread(2 * PER_GROUP, WIDTH)


def prepare(flag_ref, dt_ref, near_ref, param_ref, *refs):
    rate_ref, wide_ref, grow_ref, cum_ref, cumt_ref, slope_ref, other_ref, rows_ref = refs[-8:]
    params = param_ref[...]
    decay_rate = jnp.exp(params[0:1, :])
    raw = dt_ref[...] + params[1:2, :]
    rate, cum, tail, wide, grow = decays(raw, decay_rate)
    rate_ref[...] = rate
    wide_ref[...] = wide
    grow_ref[...] = grow
    cum_ref[...] = cum
    cumt_ref[...] = cum.T
    small = jnp.exp(-jnp.abs(raw))
    slope_ref[...] = jnp.where(raw >= 0.0, 1.0, small) / (1.0 + small)
    _, _, near_tail, near_wide, near_grow = decays(near_ref[:SPAN, :] + params[1:2, :], decay_rate)
    other_ref[...] = jnp.where(flag_ref[2] == 1, near_wide, near_grow)
    rows_ref[...] = jnp.concatenate(
        [jnp.exp(tail), decay_rate, params[2:3, :], jnp.exp(near_tail), jnp.zeros((4, H), F32)], axis=0
    )


def carry_state(
    g, carried, flag_ref, x_ref, dy_ref, b_ref, c_ref, wide_ref, grow_ref, rows_ref, spread_ref, *refs
):
    sent_ref = refs[-1]

    @pl.when(flag_ref[1] == 1)
    def _():
        forward = flag_ref[0] == 1
        heads = slice(g * PER_GROUP, (g + 1) * PER_GROUP)
        factor = jnp.where(forward, wide_ref[:, heads], grow_ref[:, heads])
        own_rows = jnp.where(
            forward, b_ref[:, g * N : (g + 1) * N], c_ref[:, g * N : (g + 1) * N]
        )
        spreader = spread_ref
        factor_hl = split(factor)
        decay_hl = split(jnp.broadcast_to(rows_ref[0:1, heads], (8, PER_GROUP)))
        for lo in range(0, WIDTH, TILE):
            lanes = slice(lo, lo + TILE)
            wide = slice(g * WIDTH + lo, g * WIDTH + lo + TILE)
            inputs = jnp.where(forward, x_ref[:, wide], dy_ref[:, wide]).astype(F32)
            weighted = (inputs * dot(factor_hl, spreader[:, lanes])).astype(BF16)
            state = dot(own_rows, weighted, TN)
            if carried:
                arrived = refs[0][:, lanes].astype(F32)
                for more in refs[1:-1]:
                    arrived = arrived + more[:, lanes].astype(F32)
                decay = dot(decay_hl, spreader[:, lanes])[0:1, :]
                state = state + arrived * decay
            sent_ref[:, lanes] = state.astype(BF16)


def pair_state(
    groups, start, flag_ref, x_ref, dy_ref, b_ref, c_ref, near_in_ref, near_rows_ref, wide_ref, grow_ref,
    other_ref, rows_ref, spread_ref, near_ref, sent_ref,
):
    onward = flag_ref[2] == 1
    for k, g in enumerate(groups):
        heads = slice(g * PER_GROUP, (g + 1) * PER_GROUP)
        rows = slice(g * N, (g + 1) * N)
        wide = slice(g * WIDTH, (g + 1) * WIDTH)
        to = slice(k * WIDTH, (k + 1) * WIDTH)
        near_in = near_in_ref[:, (g - start) * WIDTH : (g - start + 1) * WIDTH].astype(F32) * over_lanes(other_ref[:, heads], spread_ref[...])
        near_term = dot(near_rows_ref[:, rows], near_in.astype(BF16), TN)
        near_ref[:, to] = near_term.astype(BF16)

        @pl.when(flag_ref[1] == 1)
        def _(near_term=near_term, heads=heads, rows=rows, wide=wide, to=to):
            own_rows = jnp.where(onward, b_ref[:, rows], c_ref[:, rows])
            own_in = jnp.where(onward, x_ref[:, wide], dy_ref[:, wide]).astype(F32)
            factor = jnp.where(onward, wide_ref[:, heads], grow_ref[:, heads])
            own_in = (own_in * over_lanes(factor, spread_ref[...])).astype(BF16)
            decay = over_lanes(jnp.broadcast_to(rows_ref[0:1, heads], (8, PER_GROUP)), spread_ref[...])
            sent_ref[:, to] = (dot(own_rows, own_in, TN) + near_term * decay[0:1, :]).astype(BF16)


def within_block(
    g, x_ref, dy_ref, b_ref, c_ref, rate_ref, cum_ref, cumt_ref, rows_ref, spread_ref,
    outp_ref, dxp_ref, db_ref, dc_ref, gap_ref, direct_ref, skip_ref, gap_s, direct_s, skip_s,
    rate_s, skips_s,
):
    heads = slice(g * PER_GROUP, (g + 1) * PER_GROUP)
    spreader = spread_ref
    rate_s[...] = over_lanes(rate_ref[:, heads], spreader[...])
    skips_s[...] = over_lanes(jnp.broadcast_to(rows_ref[2:3, heads], (8, PER_GROUP)), spreader[...])
    at_row = lax.broadcasted_iota(jnp.int32, (SPAN, SPAN), 0)
    at_col = lax.broadcasted_iota(jnp.int32, (SPAN, SPAN), 1)
    causal = at_row >= at_col
    first = lax.broadcasted_iota(jnp.int32, (SPAN, PAIR), 1) < P_SIZE
    b_rows, c_rows = b_ref[:, g * N : (g + 1) * N], c_ref[:, g * N : (g + 1) * N]
    scores = jnp.where(causal, dot(c_rows, b_rows, NT), 0.0)
    dscores = jnp.zeros((SPAN, SPAN), F32)
    for j in range(PAIRS):
        lanes = slice(j * PAIR, (j + 1) * PAIR)
        head = g * PER_GROUP + 2 * j
        wide = slice(g * WIDTH + j * PAIR, g * WIDTH + (j + 1) * PAIR)
        x = x_ref[:, wide].astype(F32)
        dy = dy_ref[:, wide]
        rate = rate_s[:, lanes]
        skip = skips_s[0:1, lanes]
        scaled = x * rate
        both = jnp.concatenate(
            [jnp.where(first, scaled, 0.0), jnp.where(first, 0.0, scaled)], axis=0
        ).astype(BF16)
        scaled = scaled.astype(BF16).astype(F32)
        decays = [
            jnp.exp(jnp.minimum(cum_ref[:, h : h + 1] - cumt_ref[h : h + 1, :], 0.0))
            for h in (head, head + 1)
        ]
        mixing = jnp.concatenate([(scores * d).astype(BF16) for d in decays], axis=1)
        intra = dot(mixing, both)
        dmixing = dot(dy, both, NT)
        dscores = dscores + (dmixing[:, :SPAN] * decays[0] + dmixing[:, SPAN:] * decays[1])
        crossed = dot(mixing, dy, TN)
        dscaled = jnp.where(first, crossed[:SPAN], crossed[SPAN:])
        dy = dy.astype(F32)
        direct = scaled * dscaled
        outp_ref[:, lanes] = intra + skip * x
        dxp_ref[:, lanes] = dscaled * rate + skip * dy
        gap_s[:, lanes] = dy * intra - direct
        direct_s[:, lanes] = direct
        skip_s[:, lanes] = jnp.sum((dy * x).reshape(SPAN // 8, 8, PAIR), axis=0)
    dscores = jnp.where(causal, dscores, 0.0).astype(BF16)
    dc_ref[...] = dot(dscores, b_rows)
    db_ref[...] = dot(dscores, c_rows, TN)
    one = spreader[:PER_GROUP, :]
    gap_ref[...] = per_head(gap_s[...], one)
    direct_ref[...] = per_head(direct_s[...], one)
    skip_ref[...] = per_head(skip_s[...], one)


def across_blocks(
    g, place, flag_ref, x_ref, dy_ref, b_ref, c_ref, rate_ref, wide_ref, grow_ref, slope_ref, rows_ref,
    spread_ref, dbp_ref, dcp_ref, gap_ref, direct_ref, skip_ref, outp_ref, dxp_ref, near_ref, crossed_ref,
    passed_ref, *refs,
):
    last = g == G - 1
    earlier = [refs[6 * i : 6 * i + 6] for i in range(g)] if last else []
    refs = refs[6 * len(earlier) :]
    out_ref, dx_ref, db_ref, dc_ref, ddt_ref, par_ref = refs[:6]
    factor_s, decay_s, gap_s, tail_s, product_s, *more = refs[6:]
    if last:
        out_s, dx_s, rows_s, sems = more
    else:
        out_s, dx_s = out_ref, dx_ref
    forward = flag_ref[0] == 1
    inner = flag_ref[1] == 1
    heads = slice(g * PER_GROUP, (g + 1) * PER_GROUP)
    mine = slice(g * N, (g + 1) * N)

    def moves(of):
        wide, rows = pl.ds(of * WIDTH, WIDTH), pl.ds(of * N, N)
        out, dx, db, dc = (out_s, dx_s, rows_s.at[0], rows_s.at[1]) if of == g else earlier[of][:4]
        pairs = [
            (out, out_ref.at[:, wide]),
            (dx, dx_ref.at[:, wide]),
            (db, db_ref.at[:, rows]),
            (dc, dc_ref.at[:, rows]),
        ]
        return [pltpu.make_async_copy(a, b, sems.at[of, i]) for i, (a, b) in enumerate(pairs)]

    if last:
        for of in range(g):
            for move in moves(of):
                move.start()

    def work(entering, leaving):
        if entering is not None:
            factor_s[0] = over_lanes(grow_ref[:, heads], spread_ref[...])
        if leaving is not None:
            factor_s[1] = over_lanes(wide_ref[:, heads], spread_ref[...])
        b_rows, c_rows = b_ref[:, mine], c_ref[:, mine]
        db, dc = dbp_ref[...], dcp_ref[...]
        for k in range(WIDTH // TILE):
            lanes = slice(k * TILE, (k + 1) * TILE)
            wide_lanes = slice(g * WIDTH + k * TILE, g * WIDTH + (k + 1) * TILE)
            there = slice(place * WIDTH + k * TILE, place * WIDTH + (k + 1) * TILE)
            out, dx, gap = outp_ref[:, lanes], dxp_ref[:, lanes], 0.0
            if entering is not None:
                enter = entering(lanes, there)
                grow = factor_s[0, :, lanes]
                dy = dy_ref[:, wide_lanes].astype(F32)
                inter = dot(c_rows, enter) * grow
                dc = dc + dot((dy * grow).astype(BF16), enter, NT)
                out = out + inter
                gap = dy * inter
            if leaving is not None:
                leave = leaving(lanes, there)
                wide = factor_s[1, :, lanes]
                dweighted = dot(b_rows, leave)
                weighted = (x_ref[:, wide_lanes].astype(F32) * wide).astype(BF16)
                db = db + dot(weighted, leave, NT)
                dx = dx + wide * dweighted
                tail_term = weighted.astype(F32) * dweighted
                gap = gap - tail_term
                tail_s[:, lanes] = tail_term
            out_s[:, lanes] = out.astype(BF16)
            dx_s[:, lanes] = dx.astype(BF16)
            gap_s[:, lanes] = gap
            if entering is not None and leaving is not None:
                both = enter.astype(F32) * leave.astype(F32)
                product_s[:, lanes] = jnp.sum(both.reshape(N // 8, 8, TILE), axis=0)
        if leaving is None:
            tail_s[...] = jnp.zeros((SPAN, WIDTH), F32)
        if entering is None or leaving is None:
            product_s[...] = jnp.zeros((8, WIDTH), F32)
        if last:
            rows_s[0] = db
            rows_s[1] = dc
        else:
            db_ref[...] = db
            dc_ref[...] = dc

    def near_term(lanes, there):
        return near_ref[:, there]

    def far_term(lanes, there):
        return crossed_ref[:, there]

    def joined(lanes, there):
        decayed = passed_ref[:, there].astype(F32) * decay_s[0:1, lanes]
        return (decayed + near_ref[:, there].astype(F32)).astype(BF16)

    @pl.when(jnp.logical_and(inner, forward))
    def _():
        work(near_term, far_term)

    @pl.when(jnp.logical_and(inner, jnp.logical_not(forward)))
    def _():
        work(far_term, near_term)

    @pl.when(jnp.logical_not(inner))
    def _():
        decay_s[...] = over_lanes(jnp.broadcast_to(rows_ref[3:4, heads], (8, PER_GROUP)), spread_ref[...])

        @pl.when(forward)
        def _():
            work(None, joined)

        @pl.when(jnp.logical_not(forward))
        def _():
            work(joined, None)

    if last:
        for move in moves(g):
            move.start()
    one = spread_ref[:PER_GROUP, :]
    gap = gap_ref[...] + per_head(gap_s[...], one)
    tail_in = per_head(tail_s[...], one)
    product = per_head(product_s[...], one)
    rate = rate_ref[:, heads]
    decay_rate = rows_ref[1:2, heads]
    dtail = jnp.sum(tail_in, axis=0, keepdims=True) + rows_ref[0:1, heads] * jnp.sum(
        product, axis=0, keepdims=True
    )
    at_row = lax.broadcasted_iota(jnp.int32, (SPAN, SPAN), 0)
    at_col = lax.broadcasted_iota(jnp.int32, (SPAN, SPAN), 1)
    upper = jnp.where(at_row <= at_col, 1.0, 0.0)
    dlog = dot(upper, gap, precision=lax.Precision.HIGHEST) + dtail
    drate = (direct_ref[...] + tail_in) / rate - decay_rate * dlog
    ddt = drate * slope_ref[:, heads]
    da = -decay_rate * jnp.sum(rate * dlog, axis=0, keepdims=True)
    dbias = jnp.sum(ddt, axis=0, keepdims=True)
    dskip = jnp.sum(skip_ref[...], axis=0, keepdims=True)
    par = jnp.concatenate([da, dbias, dskip, jnp.zeros((5, PER_GROUP), F32)], axis=0)
    if last:
        ddt_ref[...] = jnp.concatenate([before[4][...] for before in earlier] + [ddt], axis=1)
        par_ref[...] = jnp.concatenate([before[5][...] for before in earlier] + [par], axis=1)
        for of in range(G):
            for move in moves(of):
                move.wait()
    else:
        ddt_ref[...] = ddt
        par_ref[...] = par


SCALARS = pl.BlockSpec(memory_space=pltpu.SMEM)
ANYWHERE = pl.BlockSpec(memory_space=pl.ANY)
PARAMS = pltpu.CompilerParams(vmem_limit_bytes=VMEM_LIMIT)
ON_CHIP = pl.BlockSpec(memory_space=pltpu.VMEM)


def cost(flops, moved):
    return pl.CostEstimate(flops=int(flops), bytes_accessed=int(moved), transcendentals=0)


def call_lay_out():
    return pl.pallas_call(
        lay_out,
        out_specs=ON_CHIP,
        out_shape=jax.ShapeDtypeStruct((2 * PER_GROUP, WIDTH), BF16),
        compiler_params=PARAMS,
        cost_estimate=cost(1, 1),
        name="lay_out",
    )()


def call_prepare(flags, dt_rows, near_dt, params, data):
    square = jax.ShapeDtypeStruct((SPAN, H), F32)
    return pl.pallas_call(
        prepare,
        in_specs=[SCALARS] + [ON_CHIP] * 7,
        out_specs=[ON_CHIP] * 8,
        out_shape=[square] * 7 + [jax.ShapeDtypeStruct((8, H), F32)],
        compiler_params=PARAMS,
        cost_estimate=cost(1, 1),
        name="prepare",
    )(flags, dt_rows, near_dt, params, *data)


def call_pair(groups, start, flags, data, near, prep):
    _, wide, grow, _, _, _, other, rows, spreader = prep
    state = jax.ShapeDtypeStruct((N, len(groups) * WIDTH), BF16)
    return pl.pallas_call(
        functools.partial(pair_state, groups, start),
        in_specs=[SCALARS] + [ON_CHIP] * 11,
        out_specs=[ON_CHIP] * 2,
        out_shape=[state] * 2,
        compiler_params=PARAMS,
        cost_estimate=cost(1, 1),
        name=f"pair{groups[0]}",
    )(flags, *data, *near, wide, grow, other, rows, spreader)


def call_carry(g, flags, data, prep, arrived):
    values, cot, b_rows, c_rows = data
    _, wide, grow, _, _, _, _, rows, spreader = prep
    return pl.pallas_call(
        functools.partial(carry_state, g, bool(arrived)),
        in_specs=[SCALARS] + [ON_CHIP] * (8 + len(arrived)),
        out_specs=ON_CHIP,
        out_shape=jax.ShapeDtypeStruct((N, WIDTH), BF16),
        compiler_params=PARAMS,
        cost_estimate=cost(1, 1),
        name=f"carry{g}",
    )(flags, values, cot, b_rows, c_rows, wide, grow, rows, spreader, *arrived)


def call_within(g, data, prep):
    values, cot, b_rows, c_rows = data
    rate, _, _, cum, cumt, _, _, rows, spreader = prep
    wide_shape = jax.ShapeDtypeStruct((SPAN, WIDTH), F32)
    rows_shape = jax.ShapeDtypeStruct((SPAN, N), F32)
    head_shape = jax.ShapeDtypeStruct((SPAN, PER_GROUP), F32)
    return pl.pallas_call(
        functools.partial(within_block, g),
        in_specs=[ON_CHIP] * 9,
        out_specs=[ON_CHIP] * 7,
        out_shape=[wide_shape] * 2
        + [rows_shape] * 2
        + [head_shape] * 2
        + [jax.ShapeDtypeStruct((8, PER_GROUP), F32)],
        scratch_shapes=[pltpu.VMEM((SPAN, WIDTH), F32)] * 2
        + [pltpu.VMEM((8, WIDTH), F32), pltpu.VMEM((SPAN, WIDTH), F32), pltpu.VMEM((8, WIDTH), F32)],
        compiler_params=PARAMS,
        cost_estimate=cost(1, 1),
        name=f"within{g}",
    )(values, cot, b_rows, c_rows, rate, cum, cumt, rows, spreader)


def call_across(g, place, flags, data, prep, local, states, earlier):
    values, cot, b_rows, c_rows = data
    rate, wide, grow, _, _, slope, _, rows, spreader = prep
    outp, dxp, dbp, dcp, gap, direct, skip = local
    last = g == G - 1
    groups = G if last else 1
    tokens = values.shape[0]
    before = [a for result in earlier for a in result] if last else []
    scratch = [pltpu.VMEM((2, SPAN, WIDTH), F32), pltpu.VMEM((8, WIDTH), F32)]
    scratch += [pltpu.VMEM((SPAN, WIDTH), F32)] * 2 + [pltpu.VMEM((8, WIDTH), F32)]
    if last:
        scratch += [pltpu.VMEM((SPAN, WIDTH), BF16)] * 2
        scratch += [pltpu.VMEM((2, SPAN, N), F32), pltpu.SemaphoreType.DMA((G, 4))]
    return pl.pallas_call(
        functools.partial(across_blocks, g, place),
        in_specs=[SCALARS] + [ON_CHIP] * (20 + len(before)),
        out_specs=[ANYWHERE if last else ON_CHIP] * 4 + [ON_CHIP] * 2,
        out_shape=[jax.ShapeDtypeStruct((tokens, groups * WIDTH), BF16)] * 2
        + [jax.ShapeDtypeStruct((tokens, groups * N), F32)] * 2
        + [jax.ShapeDtypeStruct((rows_, groups * PER_GROUP), F32) for rows_ in (tokens, 8)],
        scratch_shapes=scratch,
        compiler_params=PARAMS,
        cost_estimate=cost(1, 1),
        name=f"across{g}",
    )(flags, values, cot, b_rows, c_rows, rate, wide, grow, slope, rows, spreader,
      dbp, dcp, gap, direct, skip, outp, dxp, *states, *before)


def per_device(values, b_rows, c_rows, dt_rows, a_log, dt_bias, d_skip, cotangent):
    ranks = lax.axis_size("seq")
    copies = lax.axis_size("dp")
    rank = lax.axis_index("seq")
    tokens = values.shape[1]
    mine = a_log.shape[0]
    data = (
        values.reshape(tokens, H * P_SIZE),
        cotangent.reshape(tokens, H * P_SIZE),
        b_rows.reshape(tokens, G * N),
        c_rows.reshape(tokens, G * N),
    )
    own = jnp.concatenate([jnp.stack([a_log, dt_bias, d_skip]), jnp.zeros((5, mine), F32)], axis=0)
    at_lane = lax.broadcasted_iota(jnp.int32, (8, H), 1) // mine
    own = jnp.where(at_lane == rank, jnp.tile(own, (1, ranks)), 0.0)
    own_dt = dt_rows.reshape(tokens, H)
    half = ranks // 2
    forward = rank < half
    depth = jnp.where(forward, rank, ranks - 1 - rank)

    def flags(*bits):
        return jnp.stack([jnp.asarray(bit) for bit in bits]).astype(jnp.int32)

    def both_ways(step):
        return [(step, step + 1), (ranks - 1 - step, ranks - 2 - step)]

    if ranks == 4:
        marks = flags(forward, depth == 1, rank % 2 == 1)
        swap = [(i, i ^ 1) for i in range(ranks)]
        def after(value, *others):
            return lax.optimization_barrier((value, *others))[0]

        mine_dt = jnp.concatenate([own_dt, own], axis=0)
        near_dt = lax.ppermute(mine_dt, "seq", swap)
        even = rank % 2 == 0
        near_rows = lax.ppermute(jnp.where(even, data[2], data[3]), "seq", swap)

        def from_near(first, last, x, dy):
            lanes = slice(first * WIDTH, last * WIDTH)
            return lax.ppermute(jnp.where(even, x[:, lanes], dy[:, lanes]), "seq", swap)

        parts = ((0, 1), (2, 3))
        near = from_near(0, 2, data[0], data[1])
        params = own + near_dt[SPAN:]
        params = params + lax.ppermute(params, "seq", [(i, i ^ 2) for i in range(ranks)])
        prep = (*call_prepare(marks, own_dt, near_dt, params, data), call_lay_out())

        def prep_after(token):
            return (*prep[:7], after(prep[7], token), prep[8])

        pairs = [call_pair(parts[0], 0, marks, data, (near, near_rows), prep)]
        rest, _ = lax.optimization_barrier((data[:2], pairs[0][0]))
        near = from_near(2, G, *rest)
        local = [call_within(0, data, prep_after(pairs[0][0]))]
        for part in parts[1:]:
            ready = prep_after(local[0][-1] if len(pairs) == 1 else pairs[-1][0])
            pairs.append(call_pair(part, 2, marks, data, (near, near_rows), ready))
        crossed = [lax.ppermute(sent, "seq", both_ways(1)) for _, sent in pairs]
        token = pairs[-1][0]
        for g in range(1, G):
            local.append(call_within(g, data, prep_after(token)))
            token = local[g][-1]

        def pass_on(k, *tokens):
            arrived = after(crossed[k], *tokens)
            return arrived, lax.ppermute(arrived, "seq", both_ways(2))

        def finish(g, place, states, earlier):
            ready = prep_after(local[-1][-1])
            if earlier:
                ready = (*ready[:7], after(ready[7], earlier[-1][-1]), ready[8])
            return (*earlier, call_across(g, place, marks, data, ready, local[g], states, earlier))

        states = (pairs[0][0], *pass_on(0, local[1][-1]))
        results = finish(1, 1, states, finish(0, 0, states, ()))
        states = (pairs[1][0], *pass_on(1, results[-1][-1]))
        result = finish(3, 1, states, finish(2, 0, states, results))[-1]
    else:
        marks = flags(forward, True, True)
        params = lax.psum(own, "seq")
        prep = (*call_prepare(marks, own_dt, own_dt, params, data), call_lay_out())
        states = []
        for g in range(G):
            first = None
            for step in range(half):
                arrived = () if first is None else (first,)
                sent = call_carry(g, flags(forward, depth == step), data, prep, arrived)
                got = lax.ppermute(sent, "seq", both_ways(step))
                if step < half - 1:
                    first = got if first is None else first + got
            for step in range(half, ranks - 1):
                role = flags(jnp.logical_not(forward), depth == ranks - 1 - step)
                sent = call_carry(g, role, data, prep, (got,))
                got = got + lax.ppermute(sent, "seq", both_ways(step))
            states.append((jnp.zeros_like(got) if first is None else first, got, got))
        results = ()
        for g in range(G):
            local = call_within(g, data, prep)
            results += (call_across(g, 0, marks, data, prep, local, states[g], results),)
        result = results[-1]

    out, dx, db, dc, ddt, par = result
    for axis, size in (("seq", ranks), ("dp", copies)):
        hop = 1
        while hop < size:
            def swapped(bits):
                return lax.ppermute(par, axis, [(i, i ^ bits) for i in range(size)])

            if 2 * hop < size:
                par = (par + swapped(hop)) + (swapped(2 * hop) + swapped(3 * hop))
            else:
                par = par + swapped(hop)
            hop *= 4
    grad_params = lax.dynamic_slice_in_dim(par, rank * mine, mine, 1)[:3]
    return (
        out.reshape(1, tokens, H * P_SIZE),
        dx.reshape(1, tokens, H * P_SIZE),
        db.reshape(1, tokens, G * N),
        dc.reshape(1, tokens, G * N),
        ddt.reshape(1, tokens, H),
        grad_params,
    )


def solution(mesh):
    rows = P("dp", "seq", None)
    heads = P("seq")
    return jax.shard_map(
        per_device,
        mesh=mesh,
        in_specs=(rows, rows, rows, rows, heads, heads, heads, rows),
        out_specs=(rows, rows, rows, rows, rows, P(None, "seq")),
        check_vma=False,
    )
```

```python
import functools

import jax
import jax.numpy as jnp
from jax import lax
from jax.experimental import pallas as pl
from jax.experimental.pallas import tpu as pltpu
from jax.sharding import PartitionSpec as P

H = 128
G = 4
P_SIZE = 64
N = 256
SPAN = 128
PER_GROUP = H // G
WIDTH = PER_GROUP * P_SIZE
PAIR = 2 * P_SIZE
PAIRS = PER_GROUP // 2
TILE = 512
VMEM_LIMIT = 24 * 1024 * 1024

F32 = jnp.float32
BF16 = jnp.bfloat16
NN = (((1,), (0,)), ((), ()))
NT = (((1,), (1,)), ((), ()))
TN = (((0,), (0,)), ((), ()))


def dot(left, right, dims=NN, precision=None):
    return lax.dot_general(left, right, dims, precision=precision, preferred_element_type=F32)


def split(a):
    high = a.astype(BF16)
    low = (a - high.astype(F32)).astype(BF16)
    return jnp.concatenate([high, low], axis=1)


def spread(rows, width):
    head = lax.broadcasted_iota(jnp.int32, (rows, width), 0) & (PER_GROUP - 1)
    lane = lax.broadcasted_iota(jnp.int32, (rows, width), 1) >> 6
    return jnp.where(head == lane, 1.0, 0.0).astype(BF16)


def over_lanes(a, spreader):
    return dot(split(a), spreader)


def per_head(a, spreader):
    high = a.astype(BF16)
    low = (a - high.astype(F32)).astype(BF16)
    return dot(high, spreader, NT) + dot(low, spreader, NT)


def decays(raw, decay_rate):
    rate = jnp.maximum(raw, 0.0) + jnp.log1p(jnp.exp(-jnp.abs(raw)))
    at_row = lax.broadcasted_iota(jnp.int32, (SPAN, SPAN), 0)
    at_col = lax.broadcasted_iota(jnp.int32, (SPAN, SPAN), 1)
    lower = jnp.where(at_row >= at_col, 1.0, 0.0)
    cum = dot(lower, -rate * decay_rate, precision=lax.Precision.HIGHEST)
    tail = cum[SPAN - 1 : SPAN, :]
    wide = jnp.exp(jnp.minimum(tail - cum, 0.0)) * rate
    return rate, cum, tail, wide, jnp.exp(cum)


def prepare(flag_ref, dt_ref, near_ref, param_ref, *refs):
    rate_ref, wide_ref, grow_ref, cum_ref, cumt_ref, slope_ref, other_ref, rows_ref, spread_ref = refs[-9:]
    spread_ref[...] = spread(2 * PER_GROUP, WIDTH)
    params = param_ref[...]
    decay_rate = jnp.exp(params[0:1, :])
    raw = dt_ref[...] + params[1:2, :]
    rate, cum, tail, wide, grow = decays(raw, decay_rate)
    rate_ref[...] = rate
    wide_ref[...] = wide
    grow_ref[...] = grow
    cum_ref[...] = cum
    cumt_ref[...] = cum.T
    small = jnp.exp(-jnp.abs(raw))
    slope_ref[...] = jnp.where(raw >= 0.0, 1.0, small) / (1.0 + small)
    _, _, near_tail, near_wide, near_grow = decays(near_ref[:SPAN, :] + params[1:2, :], decay_rate)
    other_ref[...] = jnp.where(flag_ref[2] == 1, near_wide, near_grow)
    rows_ref[...] = jnp.concatenate(
        [jnp.exp(tail), decay_rate, params[2:3, :], jnp.exp(near_tail), jnp.zeros((4, H), F32)], axis=0
    )


def carry_state(
    g, carried, flag_ref, x_ref, dy_ref, b_ref, c_ref, wide_ref, grow_ref, rows_ref, spread_ref, *refs
):
    sent_ref = refs[-1]

    @pl.when(flag_ref[1] == 1)
    def _():
        forward = flag_ref[0] == 1
        heads = slice(g * PER_GROUP, (g + 1) * PER_GROUP)
        factor = jnp.where(forward, wide_ref[:, heads], grow_ref[:, heads])
        own_rows = jnp.where(
            forward, b_ref[:, g * N : (g + 1) * N], c_ref[:, g * N : (g + 1) * N]
        )
        spreader = spread_ref
        factor_hl = split(factor)
        decay_hl = split(jnp.broadcast_to(rows_ref[0:1, heads], (8, PER_GROUP)))
        for lo in range(0, WIDTH, TILE):
            lanes = slice(lo, lo + TILE)
            wide = slice(g * WIDTH + lo, g * WIDTH + lo + TILE)
            inputs = jnp.where(forward, x_ref[:, wide], dy_ref[:, wide]).astype(F32)
            weighted = (inputs * dot(factor_hl, spreader[:, lanes])).astype(BF16)
            state = dot(own_rows, weighted, TN)
            if carried:
                arrived = refs[0][:, lanes].astype(F32)
                for more in refs[1:-1]:
                    arrived = arrived + more[:, lanes].astype(F32)
                decay = dot(decay_hl, spreader[:, lanes])[0:1, :]
                state = state + arrived * decay
            sent_ref[:, lanes] = state.astype(BF16)


def pair_state(
    g, flag_ref, x_ref, dy_ref, b_ref, c_ref, near_in_ref, near_rows_ref, wide_ref, grow_ref,
    other_ref, rows_ref, spread_ref, near_ref, sent_ref,
):
    onward = flag_ref[2] == 1
    heads = slice(g * PER_GROUP, (g + 1) * PER_GROUP)
    rows = slice(g * N, (g + 1) * N)
    wide = slice(g * WIDTH, (g + 1) * WIDTH)
    near_in = near_in_ref[:, wide].astype(F32) * over_lanes(other_ref[:, heads], spread_ref[...])
    near_term = dot(near_rows_ref[:, rows], near_in.astype(BF16), TN)
    near_ref[...] = near_term.astype(BF16)

    @pl.when(flag_ref[1] == 1)
    def _():
        own_rows = jnp.where(onward, b_ref[:, rows], c_ref[:, rows])
        own_in = jnp.where(onward, x_ref[:, wide], dy_ref[:, wide]).astype(F32)
        factor = jnp.where(onward, wide_ref[:, heads], grow_ref[:, heads])
        own_in = (own_in * over_lanes(factor, spread_ref[...])).astype(BF16)
        decay = over_lanes(jnp.broadcast_to(rows_ref[0:1, heads], (8, PER_GROUP)), spread_ref[...])
        sent_ref[...] = (dot(own_rows, own_in, TN) + near_term * decay[0:1, :]).astype(BF16)


def within_block(
    g, x_ref, dy_ref, b_ref, c_ref, rate_ref, cum_ref, cumt_ref, rows_ref, spread_ref,
    outp_ref, dxp_ref, db_ref, dc_ref, gap_ref, direct_ref, skip_ref, gap_s, direct_s, skip_s,
    rate_s, skips_s,
):
    heads = slice(g * PER_GROUP, (g + 1) * PER_GROUP)
    spreader = spread_ref
    rate_s[...] = over_lanes(rate_ref[:, heads], spreader[...])
    skips_s[...] = over_lanes(jnp.broadcast_to(rows_ref[2:3, heads], (8, PER_GROUP)), spreader[...])
    at_row = lax.broadcasted_iota(jnp.int32, (SPAN, SPAN), 0)
    at_col = lax.broadcasted_iota(jnp.int32, (SPAN, SPAN), 1)
    causal = at_row >= at_col
    first = lax.broadcasted_iota(jnp.int32, (SPAN, PAIR), 1) < P_SIZE
    b_rows, c_rows = b_ref[:, g * N : (g + 1) * N], c_ref[:, g * N : (g + 1) * N]
    scores = jnp.where(causal, dot(c_rows, b_rows, NT), 0.0)
    dscores = jnp.zeros((SPAN, SPAN), F32)
    for j in range(PAIRS):
        lanes = slice(j * PAIR, (j + 1) * PAIR)
        head = g * PER_GROUP + 2 * j
        wide = slice(g * WIDTH + j * PAIR, g * WIDTH + (j + 1) * PAIR)
        x = x_ref[:, wide].astype(F32)
        dy = dy_ref[:, wide]
        rate = rate_s[:, lanes]
        skip = skips_s[0:1, lanes]
        scaled = x * rate
        both = jnp.concatenate(
            [jnp.where(first, scaled, 0.0), jnp.where(first, 0.0, scaled)], axis=0
        ).astype(BF16)
        scaled = scaled.astype(BF16).astype(F32)
        decays = [
            jnp.exp(jnp.minimum(cum_ref[:, h : h + 1] - cumt_ref[h : h + 1, :], 0.0))
            for h in (head, head + 1)
        ]
        mixing = jnp.concatenate([(scores * d).astype(BF16) for d in decays], axis=1)
        intra = dot(mixing, both)
        dmixing = dot(dy, both, NT)
        dscores = dscores + (dmixing[:, :SPAN] * decays[0] + dmixing[:, SPAN:] * decays[1])
        crossed = dot(mixing, dy, TN)
        dscaled = jnp.where(first, crossed[:SPAN], crossed[SPAN:])
        dy = dy.astype(F32)
        direct = scaled * dscaled
        outp_ref[:, lanes] = intra + skip * x
        dxp_ref[:, lanes] = dscaled * rate + skip * dy
        gap_s[:, lanes] = dy * intra - direct
        direct_s[:, lanes] = direct
        skip_s[:, lanes] = jnp.sum((dy * x).reshape(SPAN // 8, 8, PAIR), axis=0)
    dscores = jnp.where(causal, dscores, 0.0).astype(BF16)
    dc_ref[...] = dot(dscores, b_rows)
    db_ref[...] = dot(dscores, c_rows, TN)
    one = spreader[:PER_GROUP, :]
    gap_ref[...] = per_head(gap_s[...], one)
    direct_ref[...] = per_head(direct_s[...], one)
    skip_ref[...] = per_head(skip_s[...], one)


def across_blocks(
    g, flag_ref, x_ref, dy_ref, b_ref, c_ref, rate_ref, wide_ref, grow_ref, slope_ref, rows_ref, spread_ref,
    dbp_ref, dcp_ref, gap_ref, direct_ref, skip_ref, outp_ref, dxp_ref, near_ref, crossed_ref, passed_ref, *refs,
):
    earlier = refs[:6] if g else ()
    out_ref, dx_ref, db_ref, dc_ref, ddt_ref, par_ref = refs[len(earlier) : len(earlier) + 6]
    out_s, dx_s, rows_s, wide_s, grow_s, decay_s, gap_s, tail_s, product_s, out_sems, rows_sems = refs[len(earlier) + 6 :]
    forward = flag_ref[0] == 1
    inner = flag_ref[1] == 1

    def moves(k):
        lanes = pl.ds(k * TILE, TILE)
        wide = pl.ds(g * WIDTH + k * TILE, TILE)
        pairs = [(out_s.at[:, lanes], out_ref.at[:, wide]), (dx_s.at[:, lanes], dx_ref.at[:, wide])]
        return [pltpu.make_async_copy(a, b, out_sems.at[i, k]) for i, (a, b) in enumerate(pairs)]

    def rows_moves():
        lanes = pl.ds(g * N, N)
        pairs = [(rows_s.at[0], db_ref.at[:, lanes]), (rows_s.at[1], dc_ref.at[:, lanes])]
        return [pltpu.make_async_copy(a, b, rows_sems.at[i]) for i, (a, b) in enumerate(pairs)]

    heads = slice(g * PER_GROUP, (g + 1) * PER_GROUP)
    spreader = spread_ref
    one = spreader[:PER_GROUP, :]
    wide_s[...] = over_lanes(wide_ref[:, heads], spreader[...])
    grow_s[...] = over_lanes(grow_ref[:, heads], spreader[...])
    decay_s[...] = over_lanes(jnp.broadcast_to(rows_ref[3:4, heads], (8, PER_GROUP)), spreader[...])
    b_rows, c_rows = b_ref[:, g * N : (g + 1) * N], c_ref[:, g * N : (g + 1) * N]
    dc = dcp_ref[...]
    db = dbp_ref[...]
    for k in range(WIDTH // TILE):
        lanes = slice(k * TILE, (k + 1) * TILE)
        wide_lanes = slice(g * WIDTH + k * TILE, g * WIDTH + (k + 1) * TILE)
        near_term = near_ref[:, lanes]
        far_term = jnp.where(inner, crossed_ref[:, lanes], passed_ref[:, lanes])
        decay = decay_s[0:1, lanes]
        joined = (far_term.astype(F32) * decay + near_term.astype(F32)).astype(BF16)
        first = jnp.where(inner, near_term, jnp.zeros_like(near_term))
        second = jnp.where(inner, far_term, joined)
        enter = jnp.where(forward, first, second)
        leave = jnp.where(forward, second, first)
        x = x_ref[:, wide_lanes].astype(F32)
        dy = dy_ref[:, wide_lanes].astype(F32)
        grow = grow_s[:, lanes]
        wide = wide_s[:, lanes]
        inter = dot(c_rows, enter) * grow
        out_s[:, lanes] = (outp_ref[:, lanes] + inter).astype(BF16)
        dc = dc + dot((dy * grow).astype(BF16), enter, NT)
        dweighted = dot(b_rows, leave)
        weighted = (x * wide).astype(BF16)
        db = db + dot(weighted, leave, NT)
        dx_s[:, lanes] = (dxp_ref[:, lanes] + wide * dweighted).astype(BF16)
        for move in moves(k):
            move.start()
        tail_term = weighted.astype(F32) * dweighted
        gap_s[:, lanes] = dy * inter - tail_term
        tail_s[:, lanes] = tail_term
        both = enter.astype(F32) * leave.astype(F32)
        product_s[:, lanes] = jnp.sum(both.reshape(N // 8, 8, TILE), axis=0)
    gap = gap_ref[...] + per_head(gap_s[...], one)
    tail_in = per_head(tail_s[...], one)
    product = per_head(product_s[...], one)
    rows_s[0] = db
    rows_s[1] = dc
    for move in rows_moves():
        move.start()
    rate = rate_ref[:, heads]
    decay_rate = rows_ref[1:2, heads]
    dtail = jnp.sum(tail_in, axis=0, keepdims=True) + rows_ref[0:1, heads] * jnp.sum(
        product, axis=0, keepdims=True
    )
    at_row = lax.broadcasted_iota(jnp.int32, (SPAN, SPAN), 0)
    at_col = lax.broadcasted_iota(jnp.int32, (SPAN, SPAN), 1)
    upper = jnp.where(at_row <= at_col, 1.0, 0.0)
    dlog = dot(upper, gap, precision=lax.Precision.HIGHEST) + dtail
    drate = (direct_ref[...] + tail_in) / rate - decay_rate * dlog
    ddt = drate * slope_ref[:, heads]
    da = -decay_rate * jnp.sum(rate * dlog, axis=0, keepdims=True)
    dbias = jnp.sum(ddt, axis=0, keepdims=True)
    dskip = jnp.sum(skip_ref[...], axis=0, keepdims=True)
    pad = jnp.zeros((5, PER_GROUP), F32)
    par = jnp.concatenate([da, dbias, dskip, pad], axis=0)
    if g == 0:
        ddt_ref[...] = jnp.zeros((SPAN, H), F32)
        par_ref[...] = jnp.zeros((8, H), F32)
    else:
        ddt_ref[...] = earlier[2][...]
        par_ref[...] = earlier[3][...]
    ddt_ref[:, heads] = ddt
    par_ref[:, heads] = par
    for k in range(WIDTH // TILE):
        for move in moves(k):
            move.wait()
    for move in rows_moves():
        move.wait()


SCALARS = pl.BlockSpec(memory_space=pltpu.SMEM)
ANYWHERE = pl.BlockSpec(memory_space=pl.ANY)
PARAMS = pltpu.CompilerParams(vmem_limit_bytes=VMEM_LIMIT)
ON_CHIP = pl.BlockSpec(memory_space=pltpu.VMEM)


def cost(flops, moved):
    return pl.CostEstimate(flops=int(flops), bytes_accessed=int(moved), transcendentals=0)


def call_prepare(flags, dt_rows, near_dt, params, data):
    square = jax.ShapeDtypeStruct((SPAN, H), F32)
    return pl.pallas_call(
        prepare,
        in_specs=[SCALARS] + [ON_CHIP] * 7,
        out_specs=[ON_CHIP] * 9,
        out_shape=[square] * 7
        + [jax.ShapeDtypeStruct((8, H), F32), jax.ShapeDtypeStruct((2 * PER_GROUP, WIDTH), BF16)],
        compiler_params=PARAMS,
        cost_estimate=cost(3e7, 6e5),
        name="prepare",
    )(flags, dt_rows, near_dt, params, *data)


def call_pair(g, flags, data, near, prep):
    _, wide, grow, _, _, _, other, rows, spreader = prep
    state = jax.ShapeDtypeStruct((N, WIDTH), BF16)
    return pl.pallas_call(
        functools.partial(pair_state, g),
        in_specs=[SCALARS] + [ON_CHIP] * 11,
        out_specs=[ON_CHIP] * 2,
        out_shape=[state] * 2,
        compiler_params=PARAMS,
        cost_estimate=cost(3e8, 4e6),
        name=f"pair{g}",
    )(flags, *data, *near, wide, grow, other, rows, spreader)


def call_carry(g, flags, data, prep, arrived):
    values, cot, b_rows, c_rows = data
    _, wide, grow, _, _, _, _, rows, spreader = prep
    return pl.pallas_call(
        functools.partial(carry_state, g, bool(arrived)),
        in_specs=[SCALARS] + [ON_CHIP] * (8 + len(arrived)),
        out_specs=ON_CHIP,
        out_shape=jax.ShapeDtypeStruct((N, WIDTH), BF16),
        compiler_params=PARAMS,
        cost_estimate=cost(1.6e8, 3e6),
        name=f"carry{g}",
    )(flags, values, cot, b_rows, c_rows, wide, grow, rows, spreader, *arrived)


def call_within(g, data, prep):
    values, cot, b_rows, c_rows = data
    rate, _, _, cum, cumt, _, _, rows, spreader = prep
    wide_shape = jax.ShapeDtypeStruct((SPAN, WIDTH), F32)
    rows_shape = jax.ShapeDtypeStruct((SPAN, N), F32)
    head_shape = jax.ShapeDtypeStruct((SPAN, PER_GROUP), F32)
    return pl.pallas_call(
        functools.partial(within_block, g),
        in_specs=[ON_CHIP] * 9,
        out_specs=[ON_CHIP] * 7,
        out_shape=[wide_shape] * 2
        + [rows_shape] * 2
        + [head_shape] * 2
        + [jax.ShapeDtypeStruct((8, PER_GROUP), F32)],
        scratch_shapes=[pltpu.VMEM((SPAN, WIDTH), F32)] * 2
        + [pltpu.VMEM((8, WIDTH), F32), pltpu.VMEM((SPAN, WIDTH), F32), pltpu.VMEM((8, WIDTH), F32)],
        compiler_params=PARAMS,
        cost_estimate=cost(1.5e9, 4e6),
        name=f"within{g}",
    )(values, cot, b_rows, c_rows, rate, cum, cumt, rows, spreader)


def call_across(g, flags, data, prep, local, states, so_far):
    values, cot, b_rows, c_rows = data
    rate, wide, grow, _, _, slope, _, rows, spreader = prep
    outp, dxp, dbp, dcp, gap, direct, skip = local
    tokens, features = values.shape
    n_in = 21
    if so_far is None:
        earlier, specs, aliases = (), [], {}
    else:
        out, dx, db, dc, ddt, par = so_far
        earlier = (out, dx, ddt, par, db, dc)
        specs = [ANYWHERE, ANYWHERE, ON_CHIP, ON_CHIP, ANYWHERE, ANYWHERE]
        aliases = {n_in: 0, n_in + 1: 1, n_in + 2: 4, n_in + 3: 5, n_in + 4: 2, n_in + 5: 3}
    tiles = WIDTH // TILE
    return pl.pallas_call(
        functools.partial(across_blocks, g),
        in_specs=[SCALARS] + [ON_CHIP] * 20 + specs,
        out_specs=[ANYWHERE] * 4 + [ON_CHIP] * 2,
        out_shape=[jax.ShapeDtypeStruct((tokens, features), BF16)] * 2
        + [jax.ShapeDtypeStruct((tokens, G * N), F32)] * 2
        + [jax.ShapeDtypeStruct((tokens, H), F32), jax.ShapeDtypeStruct((8, H), F32)],
        scratch_shapes=[pltpu.VMEM((SPAN, WIDTH), BF16)] * 2
        + [pltpu.VMEM((2, SPAN, N), F32)]
        + ([pltpu.VMEM((SPAN, WIDTH), F32)] * 2 + [pltpu.VMEM((8, WIDTH), F32)]) * 2
        + [pltpu.SemaphoreType.DMA((2, tiles)), pltpu.SemaphoreType.DMA((2,))],
        input_output_aliases=aliases,
        compiler_params=PARAMS,
        cost_estimate=cost(6e8, 6e6),
        name=f"across{g}",
    )(flags, values, cot, b_rows, c_rows, rate, wide, grow, slope, rows, spreader,
      dbp, dcp, gap, direct, skip, outp, dxp, *states, *earlier)


def per_device(values, b_rows, c_rows, dt_rows, a_log, dt_bias, d_skip, cotangent):
    ranks = lax.axis_size("seq")
    copies = lax.axis_size("dp")
    rank = lax.axis_index("seq")
    tokens = values.shape[1]
    mine = a_log.shape[0]
    data = (
        values.reshape(tokens, H * P_SIZE),
        cotangent.reshape(tokens, H * P_SIZE),
        b_rows.reshape(tokens, G * N),
        c_rows.reshape(tokens, G * N),
    )
    own = jnp.concatenate([jnp.stack([a_log, dt_bias, d_skip]), jnp.zeros((5, mine), F32)], axis=0)
    at_lane = lax.broadcasted_iota(jnp.int32, (8, H), 1) // mine
    own = jnp.where(at_lane == rank, jnp.tile(own, (1, ranks)), 0.0)
    own_dt = dt_rows.reshape(tokens, H)
    half = ranks // 2
    forward = rank < half
    depth = jnp.where(forward, rank, ranks - 1 - rank)

    def flags(*bits):
        return jnp.stack([jnp.asarray(bit) for bit in bits]).astype(jnp.int32)

    def both_ways(step):
        return [(step, step + 1), (ranks - 1 - step, ranks - 2 - step)]

    if ranks == 4:
        marks = flags(forward, depth == 1, rank % 2 == 1)
        swap = [(i, i ^ 1) for i in range(ranks)]
        even = rank % 2 == 0
        near_dt = lax.ppermute(jnp.concatenate([own_dt, own], axis=0), "seq", swap)
        near = (
            lax.ppermute(jnp.where(even, data[0], data[1]), "seq", swap),
            lax.ppermute(jnp.where(even, data[2], data[3]), "seq", swap),
        )
        params = own + near_dt[SPAN:]
        params = params + lax.ppermute(params, "seq", [(i, i ^ 2) for i in range(ranks)])
        prep = call_prepare(marks, own_dt, near_dt, params, data)
        pairs = [call_pair(g, marks, data, near, prep) for g in range(G)]
        crossed = [lax.ppermute(sent, "seq", both_ways(1)) for _, sent in pairs]
        local, token, result = [], pairs[G - 1][0], None
        for g in range(G):
            rows, _ = lax.optimization_barrier((prep[7], token))
            local.append(call_within(g, data, (*prep[:7], rows, prep[8])))
            token = local[g][-1]

        def pass_on(g, token):
            arrived, _ = lax.optimization_barrier((crossed[g], token))
            return pairs[g][0], arrived, lax.ppermute(arrived, "seq", both_ways(2))

        states = [pass_on(0, prep[7]), pass_on(1, local[0][-1]), pass_on(2, local[3][-1])]
        result = call_across(0, marks, data, prep, local[0], states[0], None)
        result = call_across(1, marks, data, prep, local[1], states[1], result)
        states.append(pass_on(3, result[-1]))
        for g in (2, 3):
            result = call_across(g, marks, data, prep, local[g], states[g], result)
    else:
        marks = flags(forward, True, True)
        params = lax.psum(own, "seq")
        prep = call_prepare(marks, own_dt, own_dt, params, data)
        states = []
        for g in range(G):
            first = None
            for step in range(half):
                arrived = () if first is None else (first,)
                sent = call_carry(g, flags(forward, depth == step), data, prep, arrived)
                got = lax.ppermute(sent, "seq", both_ways(step))
                if step < half - 1:
                    first = got if first is None else first + got
            for step in range(half, ranks - 1):
                role = flags(jnp.logical_not(forward), depth == ranks - 1 - step)
                sent = call_carry(g, role, data, prep, (got,))
                got = got + lax.ppermute(sent, "seq", both_ways(step))
            states.append((jnp.zeros_like(got) if first is None else first, got, got))
        result = None
        for g in range(G):
            local = call_within(g, data, prep)
            result = call_across(g, marks, data, prep, local, states[g], result)
    out, dx, db, dc, ddt, par = result
    for axis, size in (("seq", ranks), ("dp", copies)):
        hop = 1
        while hop < size:

            def swapped(bits):
                return lax.ppermute(par, axis, [(i, i ^ bits) for i in range(size)])

            if 2 * hop < size:
                par = (par + swapped(hop)) + (swapped(2 * hop) + swapped(3 * hop))
            else:
                par = par + swapped(hop)
            hop *= 4
    grad_params = lax.dynamic_slice_in_dim(par, rank * mine, mine, 1)[:3]
    return (
        out.reshape(1, tokens, H * P_SIZE),
        dx.reshape(1, tokens, H * P_SIZE),
        db.reshape(1, tokens, G * N),
        dc.reshape(1, tokens, G * N),
        ddt.reshape(1, tokens, H),
        grad_params,
    )


def solution(mesh):
    rows = P("dp", "seq", None)
    heads = P("seq")
    return jax.shard_map(
        per_device,
        mesh=mesh,
        in_specs=(rows, rows, rows, rows, heads, heads, heads, rows),
        out_specs=(rows, rows, rows, rows, rows, P(None, "seq")),
        check_vma=False,
    )
```
